512 devices in a mesh: fsdp: 32 (over z_hi, x, core), seq: 16 (over z_lo, y).
Axes of the slice: x: 4, y: 8, z: 8 (z_hi: 4, z_lo: 2; z = z_hi * 2 + z_lo), core: 2. Of those that a mesh axis runs over, the one named last changes fastest.
Arguments:
- video_qkv: bfloat16 [32, 2048, 3, 4096], P('fsdp', 'seq'), may hold values from -6 to 6
- reference_rows: bfloat16 [32, 64, 5120], P('fsdp', 'seq'), may hold values from -150 to 150
- kv_weight: bfloat16 [5120, 2, 4096], P('fsdp', None, 'seq'), may hold values from -0.125 to 0.125
- pose_table: bfloat16 [256, 4096], P('fsdp', 'seq'), may hold values from -6 to 6
- pose_ids: int32 [32, 2048], P('fsdp', 'seq'), may hold values from 0 to 255
- frame_counts: int32 [32], P('fsdp'), may hold values from 1 to 4, as said below
Outputs:
- attended: bfloat16 [32, 2048, 4096], P('fsdp', 'seq')
The draws below stay inside these ranges and needn't reach their ends.
Inputs may be any that keep to these rules, and one draw needn't show every extreme that they name: `frame_counts`: every clip has 1 to 4 reference frames in the window, each making 16 slots live; in every draw some clip has exactly 4 and another exactly 1.
All inputs are finite; a program needn't handle non-finite values.
Results may differ from the reference program's by a relative error of at most 0.011.
Values may be sent and summed in bfloat16 or wider, within the bound.
No kernel may reach another device: no remote copies, remote signals or barrier semaphores. Data moves between devices by JAX's collectives and lax.ppermute only.
A program may use at most 64 MiB of HBM per device.

```python
import math
import jax
import jax.numpy as jnp
import numpy as np
from jax import lax

D = 5120
HEADS = 32
HD = 128
HW = 4096
VID = 2048
TPF = 16
MAXF = 4
REF = 64
POSE = 256
CLIPS = 32


def draw_video_qkv(key, part):
    first_key = jax.random.fold_in(jax.random.fold_in(key, 11), 0)
    shape = (CLIPS, VID, 3, HW)
    base_draw = jnp.clip(jax.random.normal(first_key, shape, jnp.float32), -3.0, 3.0)
    query = base_draw[:, :, 0, :] * 2.0
    keys_part = base_draw[:, :, 1, :]
    values_part = base_draw[:, :, 2, :]
    return jnp.stack([query, keys_part, values_part], axis=2).astype(jnp.bfloat16)


def draw_reference_rows(key, part):
    first_key, second_key, third_key = jax.random.split(jax.random.fold_in(key, 23), 3)
    column_scale = jnp.exp(jax.random.uniform(second_key, (D,), jnp.float32, 0.0, math.log(10.0)))
    row_scale = jnp.exp(jax.random.uniform(third_key, (CLIPS, REF, 1), jnp.float32, 0.0, math.log(3.0)))
    base_draw = jnp.clip(jax.random.normal(first_key, (CLIPS, REF, D), jnp.float32), -3.0, 3.0)
    return (base_draw * column_scale * row_scale).astype(jnp.bfloat16)


def draw_frame_counts(key, part):
    first_key, second_key, third_key = jax.random.split(jax.random.fold_in(key, 37), 3)
    counts = jax.random.randint(first_key, (CLIPS,), 1, MAXF + 1)
    largest = jax.random.randint(second_key, (), 0, CLIPS)
    smallest = (largest + jax.random.randint(third_key, (), 1, CLIPS)) % CLIPS
    counts = counts.at[largest].set(MAXF)
    counts = counts.at[smallest].set(1)
    return counts.astype(jnp.int32)


def with_ends(values, own_key, low, top_value):
    dims = values.shape
    place = [jax.random.randint(jax.random.fold_in(own_key, axis), (), 0, dims[axis]) for axis in range(len(dims))]
    values = values.at[tuple(place)].set(low)
    longest = dims.index(max(dims))
    place[longest] = (place[longest] + 1) % dims[longest]
    return values.at[tuple(place)].set(top_value)


def block_levels(key, dims, shards, low, high):
    level = 1.0
    for position, blocks in shards:
        steps = jax.random.uniform(jax.random.fold_in(jax.random.fold_in(key, 6), position), (blocks,), jnp.float32, low / len(shards), high / len(shards))
        level = level * jnp.repeat(jnp.exp(steps), dims[position] // blocks).reshape((-1,) + (1,) * (len(dims) - 1 - position))
    return level


def rank_bounds(count, slope):
    loads = [(1 << 20) // math.isqrt(standing ** slope) + 1 for standing in range(1, count + 1)]
    width = 1 + sum(loads) // (1 << 30)
    return np.cumsum(np.array([max(1, weight // width) for weight in loads]))


def skewed_ids(own_key, dims, amount, lean):
    listing = rank_bounds(amount, lean)
    ticket = jax.random.randint(jax.random.fold_in(own_key, 1), dims, 0, int(listing[amount - 1]))
    grade = jnp.searchsorted(jnp.asarray(listing, jnp.int32), ticket, side="right")
    return jax.random.permutation(jax.random.fold_in(own_key, 2), amount)[grade].astype(jnp.int32)


def scatter_about(rng, dims, spread, bound, pieces=(), held_as=jnp.bfloat16):
    factor_of = block_levels(rng, dims, pieces, -0.22, 0.18) if pieces else 1.0
    values = jax.random.normal(rng, dims, jnp.float32) * spread * factor_of
    return jnp.minimum(jnp.maximum(values, -bound), bound).astype(held_as)


def setup_inputs(seed: int = 0) -> dict:
    keys = jax.random.split(jax.random.key(seed), 7)
    return {
        "video_qkv": draw_video_qkv(jax.random.fold_in(keys[6], 71), 0),
        "reference_rows": draw_reference_rows(jax.random.fold_in(keys[6], 71), 0),
        "kv_weight": scatter_about(keys[2], (D, 2, HW), (D // 2) ** -0.5, 0.125, ((0, 32), (2, 16))),
        "pose_table": scatter_about(keys[3], (POSE, HW), 1.0, 6.0, ((0, 32), (1, 16))),
        "pose_ids": with_ends(skewed_ids(keys[4], (CLIPS, VID), POSE, 2), jax.random.fold_in(keys[4], 3), 0, POSE - 1).astype(jnp.int32),
        "frame_counts": draw_frame_counts(jax.random.fold_in(keys[6], 71), 0),
    }


def layer_norm(row_block):
    row_mean = lax.optimization_barrier(jnp.mean(row_block, axis=-1, keepdims=True))
    centered = row_block - row_mean
    row_var = lax.optimization_barrier(jnp.mean(centered * centered, axis=-1, keepdims=True))
    return centered * lax.rsqrt(row_var + 1e-06)

def head_attention(inputs):
    query_head, key_head, value_head, live_keys = inputs
    score_scale = 1.0 / math.sqrt(HD)
    scores = jnp.dot(query_head, key_head.T, preferred_element_type=jnp.float32) * score_scale
    scores = jnp.where(live_keys[None, :], scores, -1e+30)
    row_max = lax.optimization_barrier(jnp.max(scores, axis=-1, keepdims=True))
    expo = jnp.where(live_keys[None, :], jnp.exp(scores - row_max), 0.0)
    row_total = lax.optimization_barrier(jnp.sum(expo, axis=-1, keepdims=True))
    weights = (expo / row_total).astype(jnp.bfloat16)
    return jnp.dot(weights, value_head, preferred_element_type=jnp.float32).astype(jnp.bfloat16)

def clip_attention(inputs):
    query, key_rows, value_rows, count = inputs
    live_keys = jnp.arange(VID + REF, dtype=jnp.int32) < (VID + TPF * count).astype(jnp.int32)
    query_heads = query.reshape(VID, HEADS, HD).transpose(1, 0, 2)
    key_heads = key_rows.reshape(VID + REF, HEADS, HD).transpose(1, 0, 2)
    value_heads = value_rows.reshape(VID + REF, HEADS, HD).transpose(1, 0, 2)
    live_many = jnp.broadcast_to(live_keys[None, :], (HEADS, VID + REF))
    result = lax.map(head_attention, (query_heads, key_heads, value_heads, live_many))
    return result.transpose(1, 0, 2).reshape(VID, HW)

def reference(video_qkv, reference_rows, kv_weight, pose_table, pose_ids, frame_counts):
    normed = layer_norm(reference_rows.astype(jnp.float32)).astype(jnp.bfloat16)
    ref_kv = jnp.dot(normed.reshape(CLIPS * REF, D), kv_weight.reshape(D, 2 * HW), preferred_element_type=jnp.float32)
    ref_kv = ref_kv.astype(jnp.bfloat16).reshape(CLIPS, REF, 2, HW)
    pose_query = (video_qkv[:, :, 0, :].astype(jnp.float32) + pose_table[pose_ids].astype(jnp.float32)).astype(jnp.bfloat16)
    key_rows = jnp.concatenate([video_qkv[:, :, 1, :], ref_kv[:, :, 0, :]], axis=1)
    value_rows = jnp.concatenate([video_qkv[:, :, 2, :], ref_kv[:, :, 1, :]], axis=1)
    return lax.map(clip_attention, (pose_query, key_rows, value_rows, frame_counts))
```

```python
import math

import jax
import jax.numpy as jnp
from jax import lax
from jax.experimental import pallas as pl
from jax.experimental.pallas import tpu as pltpu
from jax.sharding import PartitionSpec as P

HD = 128
TPF = 16
WROWS = 176
IDROWS = 16


def fsdp_perm(move):
    pairs = []
    for i in range(32):
        z, x, c = move(i // 8, i // 2 % 4, i % 2)
        pairs.append((i, z % 4 * 8 + x % 4 * 2 + c))
    return pairs


def direction(core):
    return 1 - 2 * core


Z_RING = fsdp_perm(lambda z, x, c: (z + direction(c), x, c))
X_RING = fsdp_perm(lambda z, x, c: (z, x + direction(c), c))
CORE_SWAP = fsdp_perm(lambda z, x, c: (z, x, 1 - c))


def pack_kernel(tokens, group, x_ref, rows_ref, ids_ref, first_ref, second_ref, normed):
    @pl.when(pl.program_id(0) == 0)
    def _():
        x = rows_ref[...].astype(jnp.float32)
        mean = jnp.mean(x, axis=-1, keepdims=True)
        centered = x - mean
        var = jnp.mean(centered * centered, axis=-1, keepdims=True)
        out = centered * lax.rsqrt(var + 1e-06)
        r = x.shape[0]
        for c in range(x.shape[1] // HD):
            normed[c * r : (c + 1) * r, :] = out[:, c * HD : (c + 1) * HD]

    ids = jnp.broadcast_to(ids_ref[...].astype(jnp.float32), (IDROWS, tokens)).astype(jnp.bfloat16)
    norm = normed[...].astype(jnp.bfloat16)
    for d in range(group):
        for k in range(3):
            col = d * 2 * HD
            first_ref[d, k * tokens : (k + 1) * tokens, :] = x_ref[k, :, col : col + HD]
            second_ref[d, k * tokens : (k + 1) * tokens, :] = x_ref[k, :, col + HD : col + 2 * HD]
        first_ref[d, 3 * tokens : 3 * tokens + IDROWS, :] = ids
        first_ref[d, 3 * tokens + IDROWS :, :] = norm


def pack(video, rows, ids):
    tokens, width = video.shape[1], video.shape[2]
    n = width // (2 * HD)
    nrows = rows.shape[0] * rows.shape[1] // HD
    group = 2
    long = 3 * tokens + IDROWS + nrows
    return pl.pallas_call(
        lambda *refs: pack_kernel(tokens, group, *refs),
        grid=(n // group,),
        out_shape=(
            jax.ShapeDtypeStruct((n, long, HD), jnp.bfloat16),
            jax.ShapeDtypeStruct((n, 3 * tokens, HD), jnp.bfloat16),
        ),
        in_specs=[
            pl.BlockSpec((3, tokens, group * 2 * HD), lambda i: (0, 0, i)),
            pl.BlockSpec(rows.shape, lambda i: (0, 0)),
            pl.BlockSpec(ids.shape, lambda i: (0, 0)),
        ],
        out_specs=(
            pl.BlockSpec((group, long, HD), lambda i: (i, 0, 0)),
            pl.BlockSpec((group, 3 * tokens, HD), lambda i: (i, 0, 0)),
        ),
        scratch_shapes=[pltpu.VMEM((nrows, HD), jnp.float32)],
        cost_estimate=pl.CostEstimate(flops=1 << 20, bytes_accessed=7 << 20, transcendentals=0),
        name="pack",
    )(video, rows, ids)


def ref_kernel(x_ref, own_ref, other_ref, kv_ref, book_ref, weight, codes, sem):
    me = lax.axis_index("fsdp")
    mz, mx, mc = me // 8, me // 2 % 4, me % 2
    kdim = weight.shape[0] // 32
    copies = []
    for side, src in ((0, own_ref), (1, other_ref)):
        core = mc if side == 0 else 1 - mc
        sign = 1 - 2 * core
        for kx in range(4):
            for kz in range(4):
                z = (mz - sign * kz + 4) % 4
                x = (mx - sign * kx + 4) % 4
                f = z * 8 + x * 2 + core
                row = (kx * 4 + kz) * WROWS
                copies.append(
                    pltpu.make_async_copy(
                        src.at[pl.ds(row, kdim), :],
                        weight.at[pl.ds(pl.multiple_of(f * kdim, 16), kdim), :],
                        sem.at[len(copies)],
                    )
                )
                copies.append(
                    pltpu.make_async_copy(
                        src.at[pl.ds(row + kdim, 16), pl.ds(0, 2 * HD)],
                        codes.at[pl.ds(pl.multiple_of(f * 16, 16), 16), :],
                        sem.at[len(copies)],
                    )
                )
    for c in copies:
        c.start()
    for c in copies:
        c.wait()
    kv_ref[...] = jnp.dot(x_ref[...], weight[...], preferred_element_type=jnp.float32).astype(jnp.bfloat16)
    for f in range(32):
        book_ref[f * 8 : (f + 1) * 8, :] = codes[f * 16 : f * 16 + 8, :]


def ref_project(rows, own, other):
    n = own.shape[1]
    return pl.pallas_call(
        ref_kernel,
        out_shape=(
            jax.ShapeDtypeStruct((rows.shape[0], n), jnp.bfloat16),
            jax.ShapeDtypeStruct((256, 2 * HD), jnp.bfloat16),
        ),
        in_specs=[
            pl.BlockSpec(memory_space=pltpu.VMEM),
            pl.BlockSpec(memory_space=pl.ANY),
            pl.BlockSpec(memory_space=pl.ANY),
        ],
        out_specs=(pl.BlockSpec(memory_space=pltpu.VMEM), pl.BlockSpec(memory_space=pltpu.VMEM)),
        scratch_shapes=[
            pltpu.VMEM((rows.shape[1], n), jnp.bfloat16),
            pltpu.VMEM((512, 2 * HD), jnp.bfloat16),
            pltpu.SemaphoreType.DMA((64,)),
        ],
        cost_estimate=pl.CostEstimate(flops=1 << 29, bytes_accessed=7 << 20, transcendentals=0),
        name="ref_project",
    )(rows, own, other)


def attend_kernel(tokens, count_ref, q_ref, k_ref, v_ref, ids_ref, book_ref, rk_ref, rv_ref, o_ref):
    per = q_ref.shape[0]
    entries = book_ref.shape[0]
    parts = []
    for j in range(per):
        ids = ids_ref[j, 0:1, :].astype(jnp.float32).astype(jnp.int32)
        entry = lax.broadcasted_iota(jnp.int32, (entries, tokens), 0)
        onehot = jnp.where(entry == ids, 1.0, 0.0).astype(jnp.bfloat16)
        lookup = lax.dot_general(onehot, book_ref[...], (((0,), (0,)), ((), ())), preferred_element_type=jnp.float32)
        parts.append((q_ref[j].astype(jnp.float32) + lookup).astype(jnp.bfloat16))
    q = jnp.concatenate(parts, axis=0)
    keys = k_ref[...].reshape(-1, HD)
    values = v_ref[...].reshape(-1, HD)
    scale = math.log2(math.e) / math.sqrt(HD)
    nt = (((1,), (1,)), ((), ()))
    s1 = lax.dot_general(q, keys, nt, preferred_element_type=jnp.float32)
    s2 = lax.dot_general(q, rk_ref[...], nt, preferred_element_type=jnp.float32)
    slot = lax.broadcasted_iota(jnp.int32, s2.shape, 1)
    live = slot < TPF * count_ref[0]
    s2 = jnp.where(live, s2, -1e30)
    top = jnp.maximum(jnp.max(s1, axis=-1, keepdims=True), jnp.max(s2, axis=-1, keepdims=True))
    p1 = jnp.exp2((s1 - top) * scale)
    p2 = jnp.where(live, jnp.exp2((s2 - top) * scale), 0.0)
    total = jnp.sum(p1, axis=-1, keepdims=True) + jnp.sum(p2, axis=-1, keepdims=True)
    out = jnp.dot(p1.astype(jnp.bfloat16), values, preferred_element_type=jnp.float32)
    out = out + jnp.dot(p2.astype(jnp.bfloat16), rv_ref[...], preferred_element_type=jnp.float32)
    out = out / total
    o_ref[...] = out.astype(jnp.bfloat16).reshape(o_ref.shape)


def attend(head, tokens, count, block, id_block, book, ref_kv):
    n = block.shape[0]
    per = 2
    slots = ref_kv.shape[0]
    pairs = 2048 * 2112
    return pl.pallas_call(
        lambda *refs: attend_kernel(tokens, *refs),
        grid_spec=pltpu.PrefetchScalarGridSpec(
            num_scalar_prefetch=1,
            grid=(n // per,),
            in_specs=[
                pl.BlockSpec((per, tokens, HD), lambda i, c: (i, 0, 0)),
                pl.BlockSpec((n, tokens, HD), lambda i, c: (0, 1, 0)),
                pl.BlockSpec((n, tokens, HD), lambda i, c: (0, 2, 0)),
                pl.BlockSpec((per, IDROWS, HD), lambda i, c: (i, 3 * tokens // IDROWS, 0)),
                pl.BlockSpec((book.shape[0], HD), lambda i, c: (0, head)),
                pl.BlockSpec((slots, HD), lambda i, c: (0, head)),
                pl.BlockSpec((slots, HD), lambda i, c: (0, 2 + head)),
            ],
            out_specs=pl.BlockSpec((per, tokens, HD), lambda i, c: (i, 0, 0)),
        ),
        out_shape=jax.ShapeDtypeStruct((n, tokens, HD), jnp.bfloat16),
        cost_estimate=pl.CostEstimate(flops=pairs * HD * 4, bytes_accessed=2 << 20, transcendentals=pairs),
        name="attend",
    )(count, block, block, block, id_block, book, ref_kv, ref_kv)


def unpack_kernel(first_ref, second_ref, o_ref):
    for d in range(first_ref.shape[0]):
        col = d * 2 * HD
        o_ref[:, col : col + HD] = first_ref[d]
        o_ref[:, col + HD : col + 2 * HD] = second_ref[d]


def unpack(first, second):
    n, tokens, _ = first.shape
    group = 4
    spec = pl.BlockSpec((group, tokens, HD), lambda i: (i, 0, 0))
    return pl.pallas_call(
        unpack_kernel,
        grid=(n // group,),
        out_shape=jax.ShapeDtypeStruct((tokens, n * 2 * HD), jnp.bfloat16),
        in_specs=[spec, spec],
        out_specs=pl.BlockSpec((tokens, group * 2 * HD), lambda i: (0, i)),
        cost_estimate=pl.CostEstimate(flops=0, bytes_accessed=2 << 20, transcendentals=0),
        name="unpack",
    )(first, second)


def exchange(x):
    return lax.all_to_all(x, "seq", 0, 0, tiled=True)


def ring(block, pairs):
    parts = [block]
    for _ in range(3):
        parts.append(lax.ppermute(parts[-1], "fsdp", pairs))
    return jnp.concatenate(parts, axis=0)


def shards(video_qkv, reference_rows, kv_weight, pose_table, pose_ids, frame_counts):
    tokens = video_qkv.shape[1]
    video = jnp.transpose(video_qkv[0], (1, 0, 2))
    depth = kv_weight.shape[0]
    first, second = pack(video, reference_rows[0], pose_ids)
    first = exchange(first)
    codes = jnp.pad(pose_table, ((0, WROWS - depth - pose_table.shape[0]), (0, kv_weight.shape[2])))
    packed = jnp.concatenate([kv_weight.reshape(depth, -1), codes], axis=0)
    own = ring(ring(packed, Z_RING), X_RING)
    other = lax.ppermute(own, "fsdp", CORE_SWAP)
    second = exchange(second)
    n = first.shape[0]
    r = reference_rows.shape[1]
    rows = first[:, 3 * tokens + IDROWS :, :].reshape(n, -1, r, HD)
    rows = jnp.transpose(rows, (0, 2, 1, 3)).reshape(n * r, -1)
    ref_kv, book = ref_project(rows, own, other)
    out0 = attend(0, tokens, frame_counts, first, first, book, ref_kv)
    out1 = attend(1, tokens, frame_counts, second, first, book, ref_kv)
    return unpack(exchange(out0), exchange(out1))[None]


def solution(mesh):
    placed = (
        P("fsdp", "seq", None, None),
        P("fsdp", "seq", None),
        P("fsdp", None, "seq"),
        P("fsdp", "seq"),
        P("fsdp", "seq"),
        P("fsdp"),
    )
    return jax.shard_map(
        shards, mesh=mesh, in_specs=placed, out_specs=P("fsdp", "seq", None), check_vma=False
    )
```

```python
import math

import jax
import jax.numpy as jnp
from jax import lax
from jax.experimental import pallas as pl
from jax.experimental.pallas import tpu as pltpu
from jax.sharding import PartitionSpec as P

HD = 128
TPF = 16
WROWS = 176
IDROWS = 16


def fsdp_perm(move):
    pairs = []
    for i in range(32):
        z, x, c = move(i // 8, i // 2 % 4, i % 2)
        pairs.append((i, z % 4 * 8 + x % 4 * 2 + c))
    return pairs


def direction(core):
    return 1 - 2 * core


Z_MOVES = [fsdp_perm(lambda z, x, c, k=k: (z + k * direction(c), x, c)) for k in (1, 2, 3)]
X_AHEAD = fsdp_perm(lambda z, x, c: (z, x + direction(c), c))
X_BEHIND = fsdp_perm(lambda z, x, c: (z, x - direction(c), c))
CORE_SWAP = fsdp_perm(lambda z, x, c: (z, x, 1 - c))
LAG = 6000


def pack_first_kernel(tokens, group, x_ref, rows_ref, ids_ref, o_ref, normed):
    @pl.when(pl.program_id(0) == 0)
    def _():
        x = rows_ref[...].astype(jnp.float32)
        mean = jnp.mean(x, axis=-1, keepdims=True)
        centered = x - mean
        var = jnp.mean(centered * centered, axis=-1, keepdims=True)
        out = centered * lax.rsqrt(var + 1e-06)
        r = x.shape[0]
        for c in range(x.shape[1] // HD):
            normed[c * r : (c + 1) * r, :] = out[:, c * HD : (c + 1) * HD]

    ids = jnp.broadcast_to(ids_ref[...].astype(jnp.float32), (IDROWS, tokens)).astype(jnp.bfloat16)
    norm = normed[...].astype(jnp.bfloat16)
    for d in range(group):
        for k in range(3):
            o_ref[d, k * tokens : (k + 1) * tokens, :] = x_ref[k, :, d * 2 * HD : d * 2 * HD + HD]
        o_ref[d, 3 * tokens : 3 * tokens + IDROWS, :] = ids
        o_ref[d, 3 * tokens + IDROWS :, :] = norm

    if LAG:
        @pl.when((pl.program_id(0) == 0) & (lax.axis_index("fsdp") % 2 == 1))
        def _():
            pl.delay(LAG)


def pack_second_kernel(tokens, group, x_ref, o_ref):
    for d in range(group):
        for k in range(3):
            o_ref[d, k * tokens : (k + 1) * tokens, :] = x_ref[k, :, d * 2 * HD + HD : (d + 1) * 2 * HD]


def pack_first(video, rows, ids):
    tokens, width = video.shape[1], video.shape[2]
    n = width // (2 * HD)
    nrows = rows.shape[0] * rows.shape[1] // HD
    group = 4
    long = 3 * tokens + IDROWS + nrows
    return pl.pallas_call(
        lambda *refs: pack_first_kernel(tokens, group, *refs),
        grid=(n // group,),
        out_shape=jax.ShapeDtypeStruct((n, long, HD), jnp.bfloat16),
        in_specs=[
            pl.BlockSpec((3, tokens, group * 2 * HD), lambda i: (0, 0, i)),
            pl.BlockSpec(rows.shape, lambda i: (0, 0)),
            pl.BlockSpec(ids.shape, lambda i: (0, 0)),
        ],
        out_specs=pl.BlockSpec((group, long, HD), lambda i: (i, 0, 0)),
        scratch_shapes=[pltpu.VMEM((nrows, HD), jnp.float32)],
        cost_estimate=pl.CostEstimate(flops=1 << 20, bytes_accessed=5 << 20, transcendentals=0),
        name="pack_first",
    )(video, rows, ids)


def pack_second(video):
    tokens, width = video.shape[1], video.shape[2]
    n = width // (2 * HD)
    group = 4
    return pl.pallas_call(
        lambda *refs: pack_second_kernel(tokens, group, *refs),
        grid=(n // group,),
        out_shape=jax.ShapeDtypeStruct((n, 3 * tokens, HD), jnp.bfloat16),
        in_specs=[pl.BlockSpec((3, tokens, group * 2 * HD), lambda i: (0, 0, i))],
        out_specs=pl.BlockSpec((group, 3 * tokens, HD), lambda i: (i, 0, 0)),
        cost_estimate=pl.CostEstimate(flops=0, bytes_accessed=5 << 20, transcendentals=0),
        name="pack_second",
    )(video)


def ref_kernel(x_ref, own_ref, other_ref, kv_ref, book_ref, weight, codes, sem):
    me = lax.axis_index("fsdp")
    mz, mx, mc = me // 8, me // 2 % 4, me % 2
    kdim = weight.shape[0] // 32
    copies = []
    for side, src in ((0, own_ref), (1, other_ref)):
        core = mc if side == 0 else 1 - mc
        sign = 1 - 2 * core
        for kx in range(4):
            for kz in range(4):
                z = (mz - sign * kz + 4) % 4
                x = (mx - sign * kx + 4) % 4
                f = z * 8 + x * 2 + core
                row = (kx * 4 + kz) * WROWS
                copies.append(
                    pltpu.make_async_copy(
                        src.at[pl.ds(row, kdim), :],
                        weight.at[pl.ds(pl.multiple_of(f * kdim, 16), kdim), :],
                        sem.at[len(copies)],
                    )
                )
                copies.append(
                    pltpu.make_async_copy(
                        src.at[pl.ds(row + kdim, 16), pl.ds(0, 2 * HD)],
                        codes.at[pl.ds(pl.multiple_of(f * 16, 16), 16), :],
                        sem.at[len(copies)],
                    )
                )
    for c in copies:
        c.start()
    for c in copies:
        c.wait()
    kv_ref[...] = jnp.dot(x_ref[...], weight[...], preferred_element_type=jnp.float32).astype(jnp.bfloat16)
    for f in range(32):
        book_ref[f * 8 : (f + 1) * 8, :] = codes[f * 16 : f * 16 + 8, :]


def ref_project(rows, own, other):
    n = own.shape[1]
    return pl.pallas_call(
        ref_kernel,
        out_shape=(
            jax.ShapeDtypeStruct((rows.shape[0], n), jnp.bfloat16),
            jax.ShapeDtypeStruct((256, 2 * HD), jnp.bfloat16),
        ),
        in_specs=[
            pl.BlockSpec(memory_space=pltpu.VMEM),
            pl.BlockSpec(memory_space=pl.ANY),
            pl.BlockSpec(memory_space=pl.ANY),
        ],
        out_specs=(pl.BlockSpec(memory_space=pltpu.VMEM), pl.BlockSpec(memory_space=pltpu.VMEM)),
        scratch_shapes=[
            pltpu.VMEM((rows.shape[1], n), jnp.bfloat16),
            pltpu.VMEM((512, 2 * HD), jnp.bfloat16),
            pltpu.SemaphoreType.DMA((64,)),
        ],
        cost_estimate=pl.CostEstimate(flops=1 << 10, bytes_accessed=1 << 10, transcendentals=0),
        compiler_params=pltpu.CompilerParams(vmem_limit_bytes=10 << 20),
        name="ref_project",
    )(rows, own, other)


def attend_kernel(tokens, sub, count_ref, q_ref, k_ref, v_ref, ids_ref, book_ref, rk_ref, rv_ref, o_ref):
    entries = book_ref.shape[0]
    keys = k_ref[...].reshape(-1, HD)
    values = v_ref[...].reshape(-1, HD)
    ref_values = rv_ref[...]
    values = jnp.concatenate([values, jnp.ones_like(values)], axis=1)
    ref_values = jnp.concatenate([ref_values, jnp.ones_like(ref_values)], axis=1)
    scale = math.log2(math.e) / math.sqrt(HD)
    nt = (((1,), (1,)), ((), ()))
    for b in range(q_ref.shape[0] // sub):
        parts = []
        for j in range(b * sub, (b + 1) * sub):
            ids = ids_ref[j, 0:1, :].astype(jnp.float32).astype(jnp.int32)
            entry = lax.broadcasted_iota(jnp.int32, (entries, tokens), 0)
            onehot = jnp.where(entry == ids, 1.0, 0.0).astype(jnp.bfloat16)
            lookup = lax.dot_general(
                onehot, book_ref[...], (((0,), (0,)), ((), ())), preferred_element_type=jnp.float32
            )
            parts.append((q_ref[j].astype(jnp.float32) + lookup).astype(jnp.bfloat16))
        q = jnp.concatenate(parts, axis=0)
        s1 = lax.dot_general(q, keys, nt, preferred_element_type=jnp.float32)
        s2 = lax.dot_general(q, rk_ref[...], nt, preferred_element_type=jnp.float32)
        live = lax.broadcasted_iota(jnp.int32, s2.shape, 1) < TPF * count_ref[0]
        s2 = jnp.where(live, s2, -1e30)
        top = jnp.maximum(jnp.max(s1, axis=-1, keepdims=True), jnp.max(s2, axis=-1, keepdims=True)) * scale
        p1 = jnp.exp2(s1 * scale - top).astype(jnp.bfloat16)
        p2 = jnp.where(live, jnp.exp2(s2 * scale - top), 0.0).astype(jnp.bfloat16)
        both = jnp.dot(p1, values, preferred_element_type=jnp.float32)
        both = both + jnp.dot(p2, ref_values, preferred_element_type=jnp.float32)
        out = both[:, :HD] / both[:, HD:]
        o_ref[b * sub : (b + 1) * sub] = out.astype(jnp.bfloat16).reshape(sub, tokens, HD)


def attend(head, tokens, count, block, id_block, book, ref_kv):
    n = block.shape[0]
    per, sub = 8, 4
    slots = ref_kv.shape[0]
    return pl.pallas_call(
        lambda *refs: attend_kernel(tokens, sub, *refs),
        grid_spec=pltpu.PrefetchScalarGridSpec(
            num_scalar_prefetch=1,
            grid=(n // per,),
            in_specs=[
                pl.BlockSpec((per, tokens, HD), lambda i, c: (i, 0, 0)),
                pl.BlockSpec((n, tokens, HD), lambda i, c: (0, 1, 0)),
                pl.BlockSpec((n, tokens, HD), lambda i, c: (0, 2, 0)),
                pl.BlockSpec((per, IDROWS, HD), lambda i, c: (i, 3 * tokens // IDROWS, 0)),
                pl.BlockSpec((book.shape[0], HD), lambda i, c: (0, head)),
                pl.BlockSpec((slots, HD), lambda i, c: (0, head)),
                pl.BlockSpec((slots, HD), lambda i, c: (0, 2 + head)),
            ],
            out_specs=pl.BlockSpec((per, tokens, HD), lambda i, c: (i, 0, 0)),
        ),
        out_shape=jax.ShapeDtypeStruct((n, tokens, HD), jnp.bfloat16),
        cost_estimate=pl.CostEstimate(flops=1 << 10, bytes_accessed=1 << 10, transcendentals=0),
        compiler_params=pltpu.CompilerParams(vmem_limit_bytes=24 << 20),
        name="attend",
    )(count, block, block, block, id_block, book, ref_kv, ref_kv)


def unpack_kernel(head, r_ref, *refs):
    o_ref, sem = refs[-2:]
    copies = []
    for d in range(r_ref.shape[0]):
        col = d * 2 * HD + head * HD
        copies.append(pltpu.make_async_copy(r_ref.at[d], o_ref.at[:, pl.ds(col, HD)], sem.at[d]))
    for c in copies:
        c.start()
    for c in copies:
        c.wait()


def unpack(head, received, partial=None):
    n, tokens, _ = received.shape
    operands = (received,) if partial is None else (received, partial)
    specs = [pl.BlockSpec(memory_space=pl.ANY)] * len(operands)
    return pl.pallas_call(
        lambda *refs: unpack_kernel(head, *refs),
        out_shape=jax.ShapeDtypeStruct((tokens, n * 2 * HD), jnp.bfloat16),
        in_specs=specs,
        out_specs=pl.BlockSpec(memory_space=pl.ANY),
        input_output_aliases={} if partial is None else {1: 0},
        scratch_shapes=[pltpu.SemaphoreType.DMA((n,))],
        cost_estimate=pl.CostEstimate(flops=0, bytes_accessed=2 << 20, transcendentals=0),
        compiler_params=pltpu.CompilerParams(vmem_limit_bytes=1 << 20),
        name="unpack",
    )(*operands)


def exchange(x):
    return lax.all_to_all(x, "seq", 0, 0, tiled=True)


def move(block, pairs):
    return lax.ppermute(block, "fsdp", pairs)


def shards(video_qkv, reference_rows, kv_weight, pose_table, pose_ids, frame_counts):
    tokens = video_qkv.shape[1]
    video = jnp.transpose(video_qkv[0], (1, 0, 2))
    depth = kv_weight.shape[0]
    first = exchange(pack_first(video, reference_rows[0], pose_ids))
    second = pack_second(video)
    codes = jnp.pad(pose_table, ((0, WROWS - depth - pose_table.shape[0]), (0, kv_weight.shape[2])))
    packed = jnp.concatenate([kv_weight.reshape(depth, -1), codes], axis=0)
    column = jnp.concatenate([packed] + [move(packed, pairs) for pairs in Z_MOVES], axis=0)
    column, second = lax.optimization_barrier((column, second))
    ahead = move(column, X_AHEAD)
    behind = move(column, X_BEHIND)
    first, ahead = lax.optimization_barrier((first, ahead))
    far = move(ahead, X_AHEAD)
    own = jnp.concatenate([column, ahead, far, behind], axis=0)
    other = move(own, CORE_SWAP)
    second = exchange(second)
    n = first.shape[0]
    r = reference_rows.shape[1]
    rows = first[:, 3 * tokens + IDROWS :, :].reshape(n, -1, r, HD)
    rows = jnp.transpose(rows, (0, 2, 1, 3)).reshape(n * r, -1)
    ref_kv, book = ref_project(rows, own, other)
    out0 = attend(0, tokens, frame_counts, first, first, book, ref_kv)
    out1 = attend(1, tokens, frame_counts, second, first, book, ref_kv)
    result = unpack(0, exchange(out0))
    return unpack(1, exchange(out1), result)[None]


def solution(mesh):
    placed = (
        P("fsdp", "seq", None, None),
        P("fsdp", "seq", None),
        P("fsdp", None, "seq"),
        P("fsdp", "seq"),
        P("fsdp", "seq"),
        P("fsdp"),
    )
    return jax.shard_map(
        shards, mesh=mesh, in_specs=placed, out_specs=P("fsdp", "seq", None), check_vma=False
    )
```

```python
import math

import jax
import jax.numpy as jnp
from jax import lax
from jax.experimental import pallas as pl
from jax.experimental.pallas import tpu as pltpu
from jax.sharding import PartitionSpec as P

HD = 128
TPF = 16
WROWS = 176
IDROWS = 16


def fsdp_perm(move):
    pairs = []
    for i in range(32):
        z, x, c = move(i // 8, i // 2 % 4, i % 2)
        pairs.append((i, z % 4 * 8 + x % 4 * 2 + c))
    return pairs


def direction(core):
    return 1 - 2 * core


Z_MOVES = [fsdp_perm(lambda z, x, c, k=k: (z + k * direction(c), x, c)) for k in (1, 2, 3)]
X_AHEAD = fsdp_perm(lambda z, x, c: (z, x + direction(c), c))
X_BEHIND = fsdp_perm(lambda z, x, c: (z, x - direction(c), c))
CORE_SWAP = fsdp_perm(lambda z, x, c: (z, x, 1 - c))
def pack_kernel(tokens, x_ref, ids_ref, o_ref, held, ids, in_sem, out_sem):
    planes, _, width = held.shape
    n = o_ref.shape[0]
    loads = [pltpu.make_async_copy(x_ref.at[k], held.at[k], in_sem.at[k]) for k in range(planes)]
    for load in loads:
        load.start()
    ids[...] = jnp.broadcast_to(ids_ref[...].astype(jnp.float32), (2 * IDROWS, tokens))[0:IDROWS].astype(jnp.bfloat16)
    stores = []
    for d in range(n):
        rows = o_ref.at[d, pl.ds(planes * tokens, IDROWS), pl.ds(0, tokens)]
        stores.append(pltpu.make_async_copy(ids, rows, out_sem.at[len(stores)]))
    for k in range(planes):
        loads[k].wait()
        for d in range(n):
            part = held.at[k, :, pl.ds(d * 2 * HD, 2 * HD)]
            rows = o_ref.at[d, pl.ds(k * tokens, tokens), :]
            copy = pltpu.make_async_copy(part, rows, out_sem.at[len(stores)])
            copy.start()
            stores.append(copy)
    for copy in stores[:n]:
        copy.start()
    for copy in stores:
        copy.wait()


def pack(video, ids):
    planes, tokens, width = video.shape
    n = width // (2 * HD)
    long = planes * tokens + IDROWS
    return pl.pallas_call(
        lambda *refs: pack_kernel(tokens, *refs),
        out_shape=jax.ShapeDtypeStruct((n, long, 2 * HD), jnp.bfloat16),
        in_specs=[pl.BlockSpec(memory_space=pl.ANY), pl.BlockSpec(memory_space=pltpu.VMEM)],
        out_specs=pl.BlockSpec(memory_space=pl.ANY),
        scratch_shapes=[
            pltpu.VMEM(video.shape, jnp.bfloat16),
            pltpu.VMEM((IDROWS, tokens), jnp.bfloat16),
            pltpu.SemaphoreType.DMA((planes,)),
            pltpu.SemaphoreType.DMA(((planes + 1) * n,)),
        ],
        cost_estimate=pl.CostEstimate(flops=0, bytes_accessed=6 << 20, transcendentals=0),
        name="pack",
    )(video, ids)


def norm_kernel(x_ref, o_ref):
    x = x_ref[...].astype(jnp.float32)
    mean = jnp.mean(x, axis=-1, keepdims=True)
    centered = x - mean
    var = jnp.mean(centered * centered, axis=-1, keepdims=True)
    out = (centered * lax.rsqrt(var + 1e-06)).astype(jnp.bfloat16)
    for d in range(o_ref.shape[0]):
        o_ref[d] = out


def norm(rows, n):
    return pl.pallas_call(
        norm_kernel,
        out_shape=jax.ShapeDtypeStruct((n,) + rows.shape, jnp.bfloat16),
        compiler_params=pltpu.CompilerParams(vmem_limit_bytes=4 << 20),
        cost_estimate=pl.CostEstimate(flops=1 << 10, bytes_accessed=1 << 10, transcendentals=0),
        name="norm",
    )(rows)


def ref_kernel(rows_ref, *refs):
    pieces = refs[:8]
    kv_ref, book_ref, x, split, codes = refs[8:]
    me = lax.axis_index("fsdp")
    mz, mx, mc = me // 8, me // 2 % 4, me % 2
    kdim = split.shape[2]
    n, r, _ = rows_ref.shape
    for d in range(n):
        x[d * r : (d + 1) * r, :] = rows_ref[d].astype(jnp.float32)
    for f in range(32):
        split[f] = x[:, f * kdim : (f + 1) * kdim].astype(jnp.bfloat16)
    total = jnp.zeros(kv_ref.shape, jnp.float32)
    for p in range(8):
        core = mc if p < 4 else 1 - mc
        sign = 1 - 2 * core
        kx = p % 4
        for kz in range(4):
            f = (mz - sign * kz + 4) % 4 * 8 + (mx - sign * kx + 4) % 4 * 2 + core
            row = kz * WROWS
            total = total + jnp.dot(
                split[f], pieces[p][row : row + kdim, :], preferred_element_type=jnp.float32
            )
            codes[pl.ds(pl.multiple_of(f * 8, 8), 8), :] = pieces[p][row + kdim : row + WROWS, 0 : 2 * HD].astype(
                jnp.float32
            )[0:8]
    kv_ref[...] = total.astype(jnp.bfloat16)
    book_ref[...] = codes[...].astype(jnp.bfloat16)


def ref_project(rows, pieces, kdim):
    n = pieces[0].shape[1]
    slots = rows.shape[0] * rows.shape[1]
    return pl.pallas_call(
        ref_kernel,
        out_shape=(
            jax.ShapeDtypeStruct((slots, n), jnp.bfloat16),
            jax.ShapeDtypeStruct((256, 2 * HD), jnp.bfloat16),
        ),
        in_specs=[pl.BlockSpec(memory_space=pltpu.VMEM)] * 9,
        out_specs=(pl.BlockSpec(memory_space=pltpu.VMEM), pl.BlockSpec(memory_space=pltpu.VMEM)),
        scratch_shapes=[
            pltpu.VMEM((slots, rows.shape[2]), jnp.float32),
            pltpu.VMEM((32, slots, kdim), jnp.bfloat16),
            pltpu.VMEM((256, 2 * HD), jnp.float32),
        ],
        compiler_params=pltpu.CompilerParams(vmem_limit_bytes=16 << 20),
        cost_estimate=pl.CostEstimate(flops=1 << 10, bytes_accessed=1 << 10, transcendentals=0),
        name="ref_project",
    )(rows, *pieces)


def attend_kernel(tokens, sub, count_ref, q_ref, k_ref, v_ref, ids_ref, book_ref, rk_ref, rv_ref, o_ref):
    entries = book_ref.shape[0]
    keys = k_ref[...].reshape(-1, HD)
    values = v_ref[...].reshape(-1, HD)
    ref_values = rv_ref[...]
    values = jnp.concatenate([values, jnp.ones_like(values)], axis=1)
    ref_values = jnp.concatenate([ref_values, jnp.ones_like(ref_values)], axis=1)
    scale = math.log2(math.e) / math.sqrt(HD)
    nt = (((1,), (1,)), ((), ()))
    for b in range(q_ref.shape[0] // sub):
        parts = []
        for j in range(b * sub, (b + 1) * sub):
            ids = ids_ref[j, 0:1, :].astype(jnp.float32).astype(jnp.int32)
            entry = lax.broadcasted_iota(jnp.int32, (entries, tokens), 0)
            onehot = jnp.where(entry == ids, 1.0, 0.0).astype(jnp.bfloat16)
            lookup = lax.dot_general(
                onehot, book_ref[...], (((0,), (0,)), ((), ())), preferred_element_type=jnp.float32
            )
            parts.append((q_ref[j].astype(jnp.float32) + lookup).astype(jnp.bfloat16))
        q = jnp.concatenate(parts, axis=0)
        s1 = lax.dot_general(q, keys, nt, preferred_element_type=jnp.float32)
        s2 = lax.dot_general(q, rk_ref[...], nt, preferred_element_type=jnp.float32)
        live = lax.broadcasted_iota(jnp.int32, s2.shape, 1) < TPF * count_ref[0]
        s2 = jnp.where(live, s2, -1e30)
        top = jnp.maximum(jnp.max(s1, axis=-1, keepdims=True), jnp.max(s2, axis=-1, keepdims=True)) * scale
        p1 = jnp.exp2(s1 * scale - top).astype(jnp.bfloat16)
        p2 = jnp.where(live, jnp.exp2(s2 * scale - top), 0.0).astype(jnp.bfloat16)
        both = jnp.dot(p1, values, preferred_element_type=jnp.float32)
        both = both + jnp.dot(p2, ref_values, preferred_element_type=jnp.float32)
        out = both[:, :HD] / both[:, HD:]
        o_ref[b * sub : (b + 1) * sub] = out.astype(jnp.bfloat16).reshape(sub, tokens, HD)


def attend(tokens, block, count, book, ref_kv):
    n = block.shape[0]
    per, sub = 8, 4
    slots = ref_kv.shape[0]
    return pl.pallas_call(
        lambda *refs: attend_kernel(tokens, sub, *refs),
        grid_spec=pltpu.PrefetchScalarGridSpec(
            num_scalar_prefetch=1,
            grid=(2, n // per),
            in_specs=[
                pl.BlockSpec((per, tokens, HD), lambda h, i, c: (i, 0, h)),
                pl.BlockSpec((n, tokens, HD), lambda h, i, c: (0, 1, h)),
                pl.BlockSpec((n, tokens, HD), lambda h, i, c: (0, 2, h)),
                pl.BlockSpec((per, IDROWS, HD), lambda h, i, c: (i, 3 * tokens // IDROWS, 0)),
                pl.BlockSpec((book.shape[0], HD), lambda h, i, c: (0, h)),
                pl.BlockSpec((slots, HD), lambda h, i, c: (0, h)),
                pl.BlockSpec((slots, HD), lambda h, i, c: (0, 2 + h)),
            ],
            out_specs=pl.BlockSpec((per, tokens, HD), lambda h, i, c: (i, 0, h)),
        ),
        out_shape=jax.ShapeDtypeStruct((n, tokens, 2 * HD), jnp.bfloat16),
        compiler_params=pltpu.CompilerParams(vmem_limit_bytes=24 << 20),
        cost_estimate=pl.CostEstimate(flops=1 << 10, bytes_accessed=1 << 10, transcendentals=0),
        name="attend",
    )(count, block, block, block, block, book, ref_kv, ref_kv)


def unpack_kernel(r_ref, o_ref, sem):
    width = r_ref.shape[2]
    copies = [
        pltpu.make_async_copy(r_ref.at[d], o_ref.at[:, pl.ds(d * width, width)], sem.at[d])
        for d in range(r_ref.shape[0])
    ]
    for c in copies:
        c.start()
    for c in copies:
        c.wait()


def unpack(received):
    n, tokens, width = received.shape
    return pl.pallas_call(
        unpack_kernel,
        out_shape=jax.ShapeDtypeStruct((tokens, n * width), jnp.bfloat16),
        in_specs=[pl.BlockSpec(memory_space=pl.ANY)],
        out_specs=pl.BlockSpec(memory_space=pl.ANY),
        scratch_shapes=[pltpu.SemaphoreType.DMA((n,))],
        compiler_params=pltpu.CompilerParams(vmem_limit_bytes=1 << 20),
        cost_estimate=pl.CostEstimate(flops=0, bytes_accessed=1 << 10, transcendentals=0),
        name="unpack",
    )(received)


def exchange(x):
    return lax.all_to_all(x, "seq", 0, 0, tiled=True)


def move(block, pairs):
    return lax.ppermute(block, "fsdp", pairs)


def turn(block, step):
    return lax.ppermute(block, "seq", seq_perm(step))


def shards(video_qkv, reference_rows, kv_weight, pose_table, pose_ids, frame_counts):
    tokens = video_qkv.shape[1]
    depth = kv_weight.shape[0]
    n = lax.axis_size("seq")
    rows = exchange(norm(reference_rows[0], n))
    codes = jnp.pad(pose_table, ((0, WROWS - depth - pose_table.shape[0]), (0, kv_weight.shape[2])))
    packed = jnp.concatenate([kv_weight.reshape(depth, -1), codes], axis=0)
    column = jnp.concatenate([packed] + [move(packed, pairs) for pairs in Z_MOVES], axis=0)
    sent = pack(jnp.transpose(video_qkv[0], (1, 0, 2)), pose_ids)
    sent, column, rows = lax.optimization_barrier((sent, column, rows))
    video = exchange(sent)
    ahead, behind = move(column, X_AHEAD), move(column, X_BEHIND)
    far = move(ahead, X_AHEAD)
    own = [column, ahead, far, behind]
    pieces = own + [move(piece, CORE_SWAP) for piece in own]
    ref_kv, book = ref_project(rows, pieces, depth)
    return unpack(exchange(attend(tokens, video, frame_counts, book, ref_kv)))[None]


def solution(mesh):
    placed = (
        P("fsdp", "seq", None, None),
        P("fsdp", "seq", None),
        P("fsdp", None, "seq"),
        P("fsdp", "seq"),
        P("fsdp", "seq"),
        P("fsdp"),
    )
    return jax.shard_map(
        shards, mesh=mesh, in_specs=placed, out_specs=P("fsdp", "seq", None), check_vma=False
    )
```

```python
import math

import jax
import jax.numpy as jnp
from jax import lax
from jax.experimental import pallas as pl
from jax.experimental.pallas import tpu as pltpu
from jax.sharding import PartitionSpec as P

HD = 128
TPF = 16
WROWS = 176
SIDE = 8


def fsdp_perm(move):
    pairs = []
    for i in range(32):
        z, x, c = move(i // 8, i // 2 % 4, i % 2)
        pairs.append((i, z % 4 * 8 + x % 4 * 2 + c))
    return pairs


def direction(core):
    return 1 - 2 * core


Z_MOVES = [fsdp_perm(lambda z, x, c, k=k: (z + k * direction(c), x, c)) for k in (1, 2, 3)]
X_AHEAD = fsdp_perm(lambda z, x, c: (z, x + direction(c), c))
X_BEHIND = fsdp_perm(lambda z, x, c: (z, x - direction(c), c))
CORE_SWAP = fsdp_perm(lambda z, x, c: (z, x, 1 - c))
def pack_kernel(x_ref, rows_ref, ids_ref, o_ref, held, side32, side, in_sem, out_sem):
    planes, tokens, _ = held.shape
    n = o_ref.shape[0]
    loads = [pltpu.make_async_copy(x_ref.at[k], held.at[k], in_sem.at[k]) for k in range(planes)]
    for load in loads:
        load.start()
    x = rows_ref[...].astype(jnp.float32)
    mean = jnp.mean(x, axis=-1, keepdims=True)
    centered = x - mean
    var = jnp.mean(centered * centered, axis=-1, keepdims=True)
    out = centered * lax.rsqrt(var + 1e-06)
    r, width = x.shape
    chunks = width // (2 * HD)
    for c in range(chunks):
        side32[c * r : (c + 1) * r, :] = out[:, c * 2 * HD : (c + 1) * 2 * HD]
    ids = jnp.broadcast_to(ids_ref[...].astype(jnp.float32), (SIDE, tokens))
    side32[chunks * r :, 0:tokens] = ids
    side32[chunks * r :, tokens:] = ids
    side[...] = side32[...].astype(jnp.bfloat16)
    stores = []
    for k in range(planes):
        loads[k].wait()
        for d in range(n):
            part = held.at[k, :, pl.ds(d * 2 * HD, 2 * HD)]
            rows = o_ref.at[d, pl.ds(k * tokens, tokens), :]
            copy = pltpu.make_async_copy(part, rows, out_sem.at[len(stores)])
            copy.start()
            stores.append(copy)
    for d in range(n):
        rows = o_ref.at[d, pl.ds(planes * tokens, side.shape[0]), :]
        copy = pltpu.make_async_copy(side, rows, out_sem.at[len(stores)])
        copy.start()
        stores.append(copy)
    for copy in stores:
        copy.wait()


def pack(video, rows, ids):
    planes, tokens, width = video.shape
    n = width // (2 * HD)
    extra = rows.shape[0] * rows.shape[1] // (2 * HD) + SIDE
    return pl.pallas_call(
        pack_kernel,
        out_shape=jax.ShapeDtypeStruct((n, planes * tokens + extra, 2 * HD), jnp.bfloat16),
        in_specs=[
            pl.BlockSpec(memory_space=pl.ANY),
            pl.BlockSpec(memory_space=pltpu.VMEM),
            pl.BlockSpec(memory_space=pltpu.VMEM),
        ],
        out_specs=pl.BlockSpec(memory_space=pl.ANY),
        scratch_shapes=[
            pltpu.VMEM(video.shape, jnp.bfloat16),
            pltpu.VMEM((extra, 2 * HD), jnp.float32),
            pltpu.VMEM((extra, 2 * HD), jnp.bfloat16),
            pltpu.SemaphoreType.DMA((planes,)),
            pltpu.SemaphoreType.DMA(((planes + 1) * n,)),
        ],
        cost_estimate=pl.CostEstimate(flops=0, bytes_accessed=6 << 20, transcendentals=0),
        name="pack",
    )(video, rows, ids)


def ref_kernel(rows_ref, *refs):
    pieces = refs[:8]
    kv_ref, book_ref, x, split, codes = refs[8:]
    me = lax.axis_index("fsdp")
    mz, mx, mc = me // 8, me // 2 % 4, me % 2
    kdim = split.shape[2]
    n, chunk = rows_ref.shape[0], rows_ref.shape[2]
    r = x.shape[0] // n
    for d in range(n):
        got = rows_ref[d].astype(jnp.float32)
        for c in range(x.shape[1] // chunk):
            x[d * r : (d + 1) * r, c * chunk : (c + 1) * chunk] = got[c * r : (c + 1) * r, :]
    for f in range(32):
        split[f] = x[:, f * kdim : (f + 1) * kdim].astype(jnp.bfloat16)
    total = jnp.zeros(kv_ref.shape, jnp.float32)
    for p in range(8):
        core = mc if p < 4 else 1 - mc
        sign = 1 - 2 * core
        kx = p % 4
        for kz in range(4):
            f = (mz - sign * kz + 4) % 4 * 8 + (mx - sign * kx + 4) % 4 * 2 + core
            row = kz * WROWS
            total = total + jnp.dot(
                split[f], pieces[p][row : row + kdim, :], preferred_element_type=jnp.float32
            )
            codes[pl.ds(pl.multiple_of(f * 8, 8), 8), :] = pieces[p][row + kdim : row + WROWS, 0 : 2 * HD].astype(
                jnp.float32
            )[0:8]
    kv_ref[...] = total.astype(jnp.bfloat16)
    book_ref[...] = codes[...].astype(jnp.bfloat16)


def ref_project(rows, pieces, kdim, depth):
    n = pieces[0].shape[1]
    slots = rows.shape[0] * (rows.shape[1] - SIDE) * rows.shape[2] // depth
    return pl.pallas_call(
        ref_kernel,
        out_shape=(
            jax.ShapeDtypeStruct((slots, n), jnp.bfloat16),
            jax.ShapeDtypeStruct((256, 2 * HD), jnp.bfloat16),
        ),
        in_specs=[pl.BlockSpec(memory_space=pltpu.VMEM)] * 9,
        out_specs=(pl.BlockSpec(memory_space=pltpu.VMEM), pl.BlockSpec(memory_space=pltpu.VMEM)),
        scratch_shapes=[
            pltpu.VMEM((slots, depth), jnp.float32),
            pltpu.VMEM((32, slots, kdim), jnp.bfloat16),
            pltpu.VMEM((256, 2 * HD), jnp.float32),
        ],
        compiler_params=pltpu.CompilerParams(vmem_limit_bytes=16 << 20),
        cost_estimate=pl.CostEstimate(flops=1 << 10, bytes_accessed=1 << 10, transcendentals=0),
        name="ref_project",
    )(rows, *pieces)


def attend_kernel(tokens, sub, count_ref, q_ref, k_ref, v_ref, ids_ref, book_ref, rk_ref, rv_ref, o_ref):
    entries = book_ref.shape[0]
    keys = k_ref[...].reshape(-1, HD)
    values = v_ref[...].reshape(-1, HD)
    ref_values = rv_ref[...]
    values = jnp.concatenate([values, jnp.ones_like(values)], axis=1)
    ref_values = jnp.concatenate([ref_values, jnp.ones_like(ref_values)], axis=1)
    scale = math.log2(math.e) / math.sqrt(HD)
    nt = (((1,), (1,)), ((), ()))
    for b in range(q_ref.shape[0] // sub):
        parts = []
        for j in range(b * sub, (b + 1) * sub):
            ids = ids_ref[j, 0:1, :].astype(jnp.float32).astype(jnp.int32)
            entry = lax.broadcasted_iota(jnp.int32, (entries, tokens), 0)
            onehot = jnp.where(entry == ids, 1.0, 0.0).astype(jnp.bfloat16)
            lookup = lax.dot_general(
                onehot, book_ref[...], (((0,), (0,)), ((), ())), preferred_element_type=jnp.float32
            )
            parts.append((q_ref[j].astype(jnp.float32) + lookup).astype(jnp.bfloat16))
        q = jnp.concatenate(parts, axis=0)
        s1 = lax.dot_general(q, keys, nt, preferred_element_type=jnp.float32)
        s2 = lax.dot_general(q, rk_ref[...], nt, preferred_element_type=jnp.float32)
        live = lax.broadcasted_iota(jnp.int32, s2.shape, 1) < TPF * count_ref[0]
        s2 = jnp.where(live, s2, -1e30)
        top = jnp.maximum(jnp.max(s1, axis=-1, keepdims=True), jnp.max(s2, axis=-1, keepdims=True)) * scale
        p1 = jnp.exp2(s1 * scale - top).astype(jnp.bfloat16)
        p2 = jnp.where(live, jnp.exp2(s2 * scale - top), 0.0).astype(jnp.bfloat16)
        both = jnp.dot(p1, values, preferred_element_type=jnp.float32)
        both = both + jnp.dot(p2, ref_values, preferred_element_type=jnp.float32)
        out = both[:, :HD] / both[:, HD:]
        o_ref[b * sub : (b + 1) * sub] = out.astype(jnp.bfloat16).reshape(sub, tokens, HD)


def attend(tokens, block, rows, count, book, ref_kv):
    n = block.shape[0]
    per, sub = 8, 4
    slots = ref_kv.shape[0]
    return pl.pallas_call(
        lambda *refs: attend_kernel(tokens, sub, *refs),
        grid_spec=pltpu.PrefetchScalarGridSpec(
            num_scalar_prefetch=1,
            grid=(2, n // per),
            in_specs=[
                pl.BlockSpec((per, tokens, HD), lambda h, i, c: (i, 0, h)),
                pl.BlockSpec((n, tokens, HD), lambda h, i, c: (0, 1, h)),
                pl.BlockSpec((n, tokens, HD), lambda h, i, c: (0, 2, h)),
                pl.BlockSpec((per, SIDE, HD), lambda h, i, c: (i, rows.shape[1] // SIDE - 1, 0)),
                pl.BlockSpec((book.shape[0], HD), lambda h, i, c: (0, h)),
                pl.BlockSpec((slots, HD), lambda h, i, c: (0, h)),
                pl.BlockSpec((slots, HD), lambda h, i, c: (0, 2 + h)),
            ],
            out_specs=pl.BlockSpec((per, tokens, HD), lambda h, i, c: (i, 0, h)),
        ),
        out_shape=jax.ShapeDtypeStruct((n, tokens, 2 * HD), jnp.bfloat16),
        compiler_params=pltpu.CompilerParams(vmem_limit_bytes=24 << 20),
        cost_estimate=pl.CostEstimate(flops=1 << 10, bytes_accessed=1 << 10, transcendentals=0),
        name="attend",
    )(count, block, block, block, rows, book, ref_kv, ref_kv)


def unpack_kernel(r_ref, o_ref, sem):
    width = r_ref.shape[2]
    copies = [
        pltpu.make_async_copy(r_ref.at[d], o_ref.at[:, pl.ds(d * width, width)], sem.at[d])
        for d in range(r_ref.shape[0])
    ]
    for c in copies:
        c.start()
    for c in copies:
        c.wait()


def unpack(received):
    n, tokens, width = received.shape
    return pl.pallas_call(
        unpack_kernel,
        out_shape=jax.ShapeDtypeStruct((tokens, n * width), jnp.bfloat16),
        in_specs=[pl.BlockSpec(memory_space=pl.ANY)],
        out_specs=pl.BlockSpec(memory_space=pl.ANY),
        scratch_shapes=[pltpu.SemaphoreType.DMA((n,))],
        compiler_params=pltpu.CompilerParams(vmem_limit_bytes=1 << 20),
        cost_estimate=pl.CostEstimate(flops=0, bytes_accessed=1 << 10, transcendentals=0),
        name="unpack",
    )(received)


def exchange(x):
    return lax.all_to_all(x, "seq", 0, 0, tiled=True)


def move(block, pairs):
    return lax.ppermute(block, "fsdp", pairs)


def turn(block, step):
    return lax.ppermute(block, "seq", seq_perm(step))


def shards(video_qkv, reference_rows, kv_weight, pose_table, pose_ids, frame_counts):
    planes_rows = 3 * video_qkv.shape[1]
    tokens = video_qkv.shape[1]
    depth = kv_weight.shape[0]
    video = exchange(pack(jnp.transpose(video_qkv[0], (1, 0, 2)), reference_rows[0], pose_ids))
    codes = jnp.pad(pose_table, ((0, WROWS - depth - pose_table.shape[0]), (0, kv_weight.shape[2])))
    packed = jnp.concatenate([kv_weight.reshape(depth, -1), codes], axis=0)
    column = jnp.concatenate([packed] + [move(packed, pairs) for pairs in Z_MOVES], axis=0)
    ahead, behind = move(column, X_AHEAD), move(column, X_BEHIND)
    far = move(ahead, X_AHEAD)
    own = [column, ahead, far, behind]
    pieces = own + [move(piece, CORE_SWAP) for piece in own]
    rows = video[:, planes_rows:, :]
    ref_kv, book = ref_project(rows, pieces, depth, reference_rows.shape[2])
    return unpack(exchange(attend(tokens, video, rows, frame_counts, book, ref_kv)))[None]


def solution(mesh):
    placed = (
        P("fsdp", "seq", None, None),
        P("fsdp", "seq", None),
        P("fsdp", None, "seq"),
        P("fsdp", "seq"),
        P("fsdp", "seq"),
        P("fsdp"),
    )
    return jax.shard_map(
        shards, mesh=mesh, in_specs=placed, out_specs=P("fsdp", "seq", None), check_vma=False
    )
```

```python
import math

import jax
import jax.numpy as jnp
from jax import lax
from jax.experimental import pallas as pl
from jax.experimental.pallas import tpu as pltpu
from jax.sharding import PartitionSpec as P

HD = 128
TPF = 16
WROWS = 176
SIDE = 8


def fsdp_perm(move):
    pairs = []
    for i in range(32):
        z, x, c = move(i // 8, i // 2 % 4, i % 2)
        pairs.append((i, z % 4 * 8 + x % 4 * 2 + c))
    return pairs


def direction(core):
    return 1 - 2 * core


Z_MOVES = [fsdp_perm(lambda z, x, c, k=k: (z + k * direction(c), x, c)) for k in (1, 2, 3)]
X_AHEAD = fsdp_perm(lambda z, x, c: (z, x + direction(c), c))
X_BEHIND = fsdp_perm(lambda z, x, c: (z, x - direction(c), c))
CORE_SWAP = fsdp_perm(lambda z, x, c: (z, x, 1 - c))
def pack_kernel(x_ref, rows_hbm, ids_hbm, o_ref, held, rows_ref, ids_ref, side32, side, in_sem, out_sem):
    planes, tokens, _ = held.shape
    n = o_ref.shape[0]
    loads = [pltpu.make_async_copy(x_ref.at[k], held.at[k], in_sem.at[k]) for k in range(planes)]
    loads.append(pltpu.make_async_copy(rows_hbm, rows_ref, in_sem.at[planes]))
    loads.append(pltpu.make_async_copy(ids_hbm, ids_ref, in_sem.at[planes + 1]))
    for load in loads:
        load.start()
    stores = []
    for k in range(planes):
        loads[k].wait()
        for d in range(n):
            part = held.at[k, :, pl.ds(d * 2 * HD, 2 * HD)]
            rows = o_ref.at[d, pl.ds(k * tokens, tokens), :]
            copy = pltpu.make_async_copy(part, rows, out_sem.at[len(stores)])
            copy.start()
            stores.append(copy)
    loads[planes].wait()
    loads[planes + 1].wait()
    x = rows_ref[...].astype(jnp.float32)
    mean = jnp.mean(x, axis=-1, keepdims=True)
    centered = x - mean
    var = jnp.mean(centered * centered, axis=-1, keepdims=True)
    out = centered * lax.rsqrt(var + 1e-06)
    r, width = x.shape
    chunks = width // (2 * HD)
    for c in range(chunks):
        side32[c * r : (c + 1) * r, :] = out[:, c * 2 * HD : (c + 1) * 2 * HD]
    ids = jnp.broadcast_to(ids_ref[...].astype(jnp.float32), (SIDE, tokens))
    side32[chunks * r :, 0:tokens] = ids
    side32[chunks * r :, tokens:] = ids
    side[...] = side32[...].astype(jnp.bfloat16)
    for d in range(n):
        rows = o_ref.at[d, pl.ds(planes * tokens, side.shape[0]), :]
        copy = pltpu.make_async_copy(side, rows, out_sem.at[len(stores)])
        copy.start()
        stores.append(copy)
    for copy in stores:
        copy.wait()


def pack(video, rows, ids):
    planes, tokens, width = video.shape
    n = width // (2 * HD)
    extra = rows.shape[0] * rows.shape[1] // (2 * HD) + SIDE
    return pl.pallas_call(
        pack_kernel,
        out_shape=jax.ShapeDtypeStruct((n, planes * tokens + extra, 2 * HD), jnp.bfloat16),
        in_specs=[pl.BlockSpec(memory_space=pl.ANY)] * 3,
        out_specs=pl.BlockSpec(memory_space=pl.ANY),
        scratch_shapes=[
            pltpu.VMEM(video.shape, jnp.bfloat16),
            pltpu.VMEM(rows.shape, jnp.bfloat16),
            pltpu.VMEM(ids.shape, jnp.int32),
            pltpu.VMEM((extra, 2 * HD), jnp.float32),
            pltpu.VMEM((extra, 2 * HD), jnp.bfloat16),
            pltpu.SemaphoreType.DMA((planes + 2,)),
            pltpu.SemaphoreType.DMA(((planes + 1) * n,)),
        ],
        cost_estimate=pl.CostEstimate(flops=0, bytes_accessed=6 << 20, transcendentals=0),
        name="pack",
    )(video, rows, ids)


def ref_kernel(block_ref, *refs):
    kv_ref, book_ref, rows_ref, held, x, split, codes, sem, piece_sem = refs[8:]
    extra = rows_ref.shape[1]
    load = pltpu.make_async_copy(block_ref.at[:, pl.ds(block_ref.shape[1] - extra, extra), :], rows_ref, sem)
    load.start()
    fetches = [pltpu.make_async_copy(refs[p], held.at[p], piece_sem.at[p]) for p in range(8)]
    for fetch in fetches:
        fetch.start()
    me = lax.axis_index("fsdp")
    mz, mx, mc = me // 8, me // 2 % 4, me % 2
    kdim = split.shape[2]
    load.wait()
    n, chunk = rows_ref.shape[0], rows_ref.shape[2]
    r = x.shape[0] // n
    for d in range(n):
        got = rows_ref[d].astype(jnp.float32)
        for c in range(x.shape[1] // chunk):
            x[d * r : (d + 1) * r, c * chunk : (c + 1) * chunk] = got[c * r : (c + 1) * r, :]
    for f in range(32):
        split[f] = x[:, f * kdim : (f + 1) * kdim].astype(jnp.bfloat16)
    total = jnp.zeros(kv_ref.shape, jnp.float32)
    for p in range(8):
        fetches[p].wait()
        core = mc if p < 4 else 1 - mc
        sign = 1 - 2 * core
        kx = p % 4
        for kz in range(4):
            f = (mz - sign * kz + 4) % 4 * 8 + (mx - sign * kx + 4) % 4 * 2 + core
            row = kz * WROWS
            total = total + jnp.dot(
                split[f], held[p, row : row + kdim, :], preferred_element_type=jnp.float32
            )
            codes[pl.ds(pl.multiple_of(f * 8, 8), 8), :] = held[p, row + kdim : row + WROWS, 0 : 2 * HD].astype(
                jnp.float32
            )[0:8]
    kv_ref[...] = total.astype(jnp.bfloat16)
    book_ref[...] = codes[...].astype(jnp.bfloat16)


def ref_project(block, pieces, kdim, r, depth):
    n = pieces[0].shape[1]
    slots = block.shape[0] * r
    extra = r * depth // block.shape[2] + SIDE
    return pl.pallas_call(
        ref_kernel,
        out_shape=(
            jax.ShapeDtypeStruct((slots, n), jnp.bfloat16),
            jax.ShapeDtypeStruct((256, 2 * HD), jnp.bfloat16),
        ),
        in_specs=[pl.BlockSpec(memory_space=pl.ANY)] * 9,
        out_specs=(pl.BlockSpec(memory_space=pltpu.VMEM), pl.BlockSpec(memory_space=pltpu.VMEM)),
        scratch_shapes=[
            pltpu.VMEM((block.shape[0], extra, block.shape[2]), jnp.bfloat16),
            pltpu.VMEM((8,) + pieces[0].shape, jnp.bfloat16),
            pltpu.VMEM((slots, depth), jnp.float32),
            pltpu.VMEM((32, slots, kdim), jnp.bfloat16),
            pltpu.VMEM((256, 2 * HD), jnp.float32),
            pltpu.SemaphoreType.DMA,
            pltpu.SemaphoreType.DMA((8,)),
        ],
        compiler_params=pltpu.CompilerParams(vmem_limit_bytes=60 << 20),
        cost_estimate=pl.CostEstimate(flops=1 << 10, bytes_accessed=1 << 10, transcendentals=0),
        name="ref_project",
    )(block, *pieces)


def attend_kernel(tokens, sub, count_ref, q_ref, k_ref, v_ref, ids_ref, book_ref, rk_ref, rv_ref, o_ref):
    entries = book_ref.shape[0]
    keys = k_ref[...].reshape(-1, HD)
    values = v_ref[...].reshape(-1, HD)
    ref_values = rv_ref[...]
    values = jnp.concatenate([values, jnp.ones_like(values)], axis=1)
    ref_values = jnp.concatenate([ref_values, jnp.ones_like(ref_values)], axis=1)
    scale = math.log2(math.e) / math.sqrt(HD)
    nt = (((1,), (1,)), ((), ()))
    for b in range(q_ref.shape[0] // sub):
        parts = []
        for j in range(b * sub, (b + 1) * sub):
            ids = ids_ref[j, 0:1, :].astype(jnp.float32).astype(jnp.int32)
            entry = lax.broadcasted_iota(jnp.int32, (entries, tokens), 0)
            onehot = jnp.where(entry == ids, 1.0, 0.0).astype(jnp.bfloat16)
            lookup = lax.dot_general(
                onehot, book_ref[...], (((0,), (0,)), ((), ())), preferred_element_type=jnp.float32
            )
            parts.append((q_ref[j].astype(jnp.float32) + lookup).astype(jnp.bfloat16))
        q = jnp.concatenate(parts, axis=0)
        s1 = lax.dot_general(q, keys, nt, preferred_element_type=jnp.float32)
        s2 = lax.dot_general(q, rk_ref[...], nt, preferred_element_type=jnp.float32)
        live = lax.broadcasted_iota(jnp.int32, s2.shape, 1) < TPF * count_ref[0]
        s2 = jnp.where(live, s2, -1e30)
        top = jnp.maximum(jnp.max(s1, axis=-1, keepdims=True), jnp.max(s2, axis=-1, keepdims=True)) * scale
        p1 = jnp.exp2(s1 * scale - top).astype(jnp.bfloat16)
        p2 = jnp.where(live, jnp.exp2(s2 * scale - top), 0.0).astype(jnp.bfloat16)
        both = jnp.dot(p1, values, preferred_element_type=jnp.float32)
        both = both + jnp.dot(p2, ref_values, preferred_element_type=jnp.float32)
        out = both[:, :HD] / both[:, HD:]
        o_ref[b * sub : (b + 1) * sub] = out.astype(jnp.bfloat16).reshape(sub, tokens, HD)


def attend(tokens, block, count, book, ref_kv):
    n = block.shape[0]
    per, sub = 16, 8
    slots = ref_kv.shape[0]
    return pl.pallas_call(
        lambda *refs: attend_kernel(tokens, sub, *refs),
        grid_spec=pltpu.PrefetchScalarGridSpec(
            num_scalar_prefetch=1,
            grid=(2, n // per),
            in_specs=[
                pl.BlockSpec((per, tokens, HD), lambda h, i, c: (i, 0, h)),
                pl.BlockSpec((n, tokens, HD), lambda h, i, c: (0, 1, h)),
                pl.BlockSpec((n, tokens, HD), lambda h, i, c: (0, 2, h)),
                pl.BlockSpec((per, SIDE, HD), lambda h, i, c: (i, block.shape[1] // SIDE - 1, 0)),
                pl.BlockSpec((book.shape[0], HD), lambda h, i, c: (0, h)),
                pl.BlockSpec((slots, HD), lambda h, i, c: (0, h)),
                pl.BlockSpec((slots, HD), lambda h, i, c: (0, 2 + h)),
            ],
            out_specs=pl.BlockSpec((per, tokens, HD), lambda h, i, c: (i, 0, h)),
        ),
        out_shape=jax.ShapeDtypeStruct((n, tokens, 2 * HD), jnp.bfloat16),
        compiler_params=pltpu.CompilerParams(vmem_limit_bytes=32 << 20),
        cost_estimate=pl.CostEstimate(flops=1 << 10, bytes_accessed=1 << 10, transcendentals=0),
        name="attend",
    )(count, block, block, block, block, book, ref_kv, ref_kv)


def unpack_kernel(r_ref, o_ref, sem):
    width = r_ref.shape[2]
    copies = [
        pltpu.make_async_copy(r_ref.at[d], o_ref.at[:, pl.ds(d * width, width)], sem.at[d])
        for d in range(r_ref.shape[0])
    ]
    for c in copies:
        c.start()
    for c in copies:
        c.wait()


def unpack(received):
    n, tokens, width = received.shape
    return pl.pallas_call(
        unpack_kernel,
        out_shape=jax.ShapeDtypeStruct((tokens, n * width), jnp.bfloat16),
        in_specs=[pl.BlockSpec(memory_space=pl.ANY)],
        out_specs=pl.BlockSpec(memory_space=pl.ANY),
        scratch_shapes=[pltpu.SemaphoreType.DMA((n,))],
        compiler_params=pltpu.CompilerParams(vmem_limit_bytes=1 << 20),
        cost_estimate=pl.CostEstimate(flops=0, bytes_accessed=1 << 10, transcendentals=0),
        name="unpack",
    )(received)


def exchange(x):
    return lax.all_to_all(x, "seq", 0, 0, tiled=True)


def move(block, pairs):
    return lax.ppermute(block, "fsdp", pairs)


def turn(block, step):
    return lax.ppermute(block, "seq", seq_perm(step))


def shards(video_qkv, reference_rows, kv_weight, pose_table, pose_ids, frame_counts):
    tokens = video_qkv.shape[1]
    depth = kv_weight.shape[0]
    video = exchange(pack(jnp.transpose(video_qkv[0], (1, 0, 2)), reference_rows[0], pose_ids))
    codes = jnp.pad(pose_table, ((0, WROWS - depth - pose_table.shape[0]), (0, kv_weight.shape[2])))
    packed = jnp.concatenate([kv_weight.reshape(depth, -1), codes], axis=0)
    column = jnp.concatenate([packed] + [move(packed, pairs) for pairs in Z_MOVES], axis=0)
    ahead, behind = move(column, X_AHEAD), move(column, X_BEHIND)
    far = move(ahead, X_AHEAD)
    own = [column, ahead, far, behind]
    pieces = own + [move(piece, CORE_SWAP) for piece in own]
    ref_kv, book = ref_project(video, pieces, depth, *reference_rows.shape[1:])
    return unpack(exchange(attend(tokens, video, frame_counts, book, ref_kv)))[None]


def solution(mesh):
    placed = (
        P("fsdp", "seq", None, None),
        P("fsdp", "seq", None),
        P("fsdp", None, "seq"),
        P("fsdp", "seq"),
        P("fsdp", "seq"),
        P("fsdp"),
    )
    return jax.shard_map(
        shards, mesh=mesh, in_specs=placed, out_specs=P("fsdp", "seq", None), check_vma=False
    )
```

```python
import math

import jax
import jax.numpy as jnp
from jax import lax
from jax.experimental import pallas as pl
from jax.experimental.pallas import tpu as pltpu
from jax.sharding import PartitionSpec as P

HD = 128
TPF = 16
WROWS = 176
SIDE = 8


def fsdp_perm(move):
    pairs = []
    for i in range(32):
        z, x, c = move(i // 8, i // 2 % 4, i % 2)
        pairs.append((i, z % 4 * 8 + x % 4 * 2 + c))
    return pairs


def direction(core):
    return 1 - 2 * core


Z_MOVES = [fsdp_perm(lambda z, x, c, k=k: (z + k * direction(c), x, c)) for k in (1, 2, 3)]
X_AHEAD = fsdp_perm(lambda z, x, c: (z, x + direction(c), c))
X_BEHIND = fsdp_perm(lambda z, x, c: (z, x - direction(c), c))
CORE_SWAP = fsdp_perm(lambda z, x, c: (z, x, 1 - c))
def pack_kernel(x_ref, rows_hbm, ids_hbm, o_ref, held, rows_ref, ids_ref, side32, side, in_sem, out_sem):
    planes, tokens, _ = held.shape
    n = o_ref.shape[0]
    loads = [pltpu.make_async_copy(x_ref.at[k], held.at[k], in_sem.at[k]) for k in range(planes)]
    loads.append(pltpu.make_async_copy(rows_hbm, rows_ref, in_sem.at[planes]))
    loads.append(pltpu.make_async_copy(ids_hbm, ids_ref, in_sem.at[planes + 1]))
    for load in loads:
        load.start()
    stores = []
    for k in range(planes):
        loads[k].wait()
        for d in range(n):
            part = held.at[k, :, pl.ds(d * 2 * HD, 2 * HD)]
            rows = o_ref.at[d, pl.ds(k * tokens, tokens), :]
            copy = pltpu.make_async_copy(part, rows, out_sem.at[len(stores)])
            copy.start()
            stores.append(copy)
    loads[planes].wait()
    loads[planes + 1].wait()
    x = rows_ref[...].astype(jnp.float32)
    mean = jnp.mean(x, axis=-1, keepdims=True)
    centered = x - mean
    var = jnp.mean(centered * centered, axis=-1, keepdims=True)
    out = centered * lax.rsqrt(var + 1e-06)
    r, width = x.shape
    chunks = width // (2 * HD)
    for c in range(chunks):
        side32[c * r : (c + 1) * r, :] = out[:, c * 2 * HD : (c + 1) * 2 * HD]
    ids = jnp.broadcast_to(ids_ref[...].astype(jnp.float32), (SIDE, tokens))
    side32[chunks * r :, 0:tokens] = ids
    side32[chunks * r :, tokens:] = ids
    side[...] = side32[...].astype(jnp.bfloat16)
    for d in range(n):
        rows = o_ref.at[d, pl.ds(planes * tokens, side.shape[0]), :]
        copy = pltpu.make_async_copy(side, rows, out_sem.at[len(stores)])
        copy.start()
        stores.append(copy)
    for copy in stores:
        copy.wait()


def pack(video, rows, ids):
    planes, tokens, width = video.shape
    n = width // (2 * HD)
    extra = rows.shape[0] * rows.shape[1] // (2 * HD) + SIDE
    return pl.pallas_call(
        pack_kernel,
        out_shape=jax.ShapeDtypeStruct((n, planes * tokens + extra, 2 * HD), jnp.bfloat16),
        in_specs=[pl.BlockSpec(memory_space=pl.ANY)] * 3,
        out_specs=pl.BlockSpec(memory_space=pl.ANY),
        scratch_shapes=[
            pltpu.VMEM(video.shape, jnp.bfloat16),
            pltpu.VMEM(rows.shape, jnp.bfloat16),
            pltpu.VMEM(ids.shape, jnp.int32),
            pltpu.VMEM((extra, 2 * HD), jnp.float32),
            pltpu.VMEM((extra, 2 * HD), jnp.bfloat16),
            pltpu.SemaphoreType.DMA((planes + 2,)),
            pltpu.SemaphoreType.DMA(((planes + 1) * n,)),
        ],
        cost_estimate=pl.CostEstimate(flops=0, bytes_accessed=6 << 20, transcendentals=0),
        name="pack",
    )(video, rows, ids)


def assemble_kernel(*refs):
    pieces = refs[:8]
    weight_ref, book_ref, codes, sem = refs[8:]
    me = lax.axis_index("fsdp")
    mz, mx, mc = me // 8, me // 2 % 4, me % 2
    kdim = weight_ref.shape[0] // 32
    copies = []
    for p in range(8):
        core = mc if p < 4 else 1 - mc
        sign = 1 - 2 * core
        kx = p % 4
        for kz in range(4):
            f = (mz - sign * kz + 4) % 4 * 8 + (mx - sign * kx + 4) % 4 * 2 + core
            row = kz * WROWS
            copy = pltpu.make_async_copy(
                pieces[p].at[pl.ds(row, kdim), :],
                weight_ref.at[pl.ds(pl.multiple_of(f * kdim, 16), kdim), :],
                sem.at[len(copies)],
            )
            copy.start()
            copies.append(copy)
            copy = pltpu.make_async_copy(
                pieces[p].at[pl.ds(row + kdim, WROWS - kdim), pl.ds(0, 2 * HD)],
                codes.at[pl.ds(pl.multiple_of(f * 16, 16), 16), :],
                sem.at[len(copies)],
            )
            copy.start()
            copies.append(copy)
    for copy in copies:
        copy.wait()
    for f in range(32):
        book_ref[f * 8 : (f + 1) * 8, :] = codes[f * 16 : f * 16 + 8, :]


def assemble(pieces, kdim):
    n = pieces[0].shape[1]
    return pl.pallas_call(
        assemble_kernel,
        out_shape=(
            jax.ShapeDtypeStruct((32 * kdim, n), jnp.bfloat16),
            jax.ShapeDtypeStruct((256, 2 * HD), jnp.bfloat16),
        ),
        in_specs=[pl.BlockSpec(memory_space=pl.ANY)] * 8,
        out_specs=(pl.BlockSpec(memory_space=pltpu.VMEM), pl.BlockSpec(memory_space=pltpu.VMEM)),
        scratch_shapes=[pltpu.VMEM((32 * 16, 2 * HD), jnp.bfloat16), pltpu.SemaphoreType.DMA((64,))],
        compiler_params=pltpu.CompilerParams(vmem_limit_bytes=8 << 20),
        cost_estimate=pl.CostEstimate(flops=1 << 10, bytes_accessed=1 << 10, transcendentals=0),
        name="assemble",
    )(*pieces)


def project_kernel(block_ref, weight_hbm, kv_ref, rows_ref, weight_ref, x, sem, weight_sem):
    extra = rows_ref.shape[1]
    load = pltpu.make_async_copy(block_ref.at[:, pl.ds(block_ref.shape[1] - extra, extra), :], rows_ref, sem)
    load.start()
    fetch = pltpu.make_async_copy(weight_hbm, weight_ref, weight_sem)
    fetch.start()
    load.wait()
    n, chunk = rows_ref.shape[0], rows_ref.shape[2]
    r = x.shape[0] // n
    for d in range(n):
        got = rows_ref[d].astype(jnp.float32)
        for c in range(x.shape[1] // chunk):
            x[d * r : (d + 1) * r, c * chunk : (c + 1) * chunk] = got[c * r : (c + 1) * r, :]
    fetch.wait()
    kv_ref[...] = jnp.dot(
        x[...].astype(jnp.bfloat16), weight_ref[...], preferred_element_type=jnp.float32
    ).astype(jnp.bfloat16)


def project(block, weight, r):
    depth, n = weight.shape
    slots = block.shape[0] * r
    extra = r * depth // block.shape[2] + SIDE
    return pl.pallas_call(
        project_kernel,
        out_shape=jax.ShapeDtypeStruct((slots, n), jnp.bfloat16),
        in_specs=[pl.BlockSpec(memory_space=pl.ANY)] * 2,
        out_specs=pl.BlockSpec(memory_space=pltpu.VMEM),
        scratch_shapes=[
            pltpu.VMEM((block.shape[0], extra, block.shape[2]), jnp.bfloat16),
            pltpu.VMEM(weight.shape, jnp.bfloat16),
            pltpu.VMEM((slots, depth), jnp.float32),
            pltpu.SemaphoreType.DMA,
            pltpu.SemaphoreType.DMA,
        ],
        compiler_params=pltpu.CompilerParams(vmem_limit_bytes=60 << 20),
        cost_estimate=pl.CostEstimate(flops=1 << 10, bytes_accessed=1 << 10, transcendentals=0),
        name="project",
    )(block, weight)


def attend_kernel(tokens, sub, count_ref, q_ref, k_ref, v_ref, ids_ref, book_ref, rk_ref, rv_ref, o_ref):
    entries = book_ref.shape[0]
    keys = k_ref[...].reshape(-1, HD)
    values = v_ref[...].reshape(-1, HD)
    ref_values = rv_ref[...]
    values = jnp.concatenate([values, jnp.ones_like(values)], axis=1)
    ref_values = jnp.concatenate([ref_values, jnp.ones_like(ref_values)], axis=1)
    scale = math.log2(math.e) / math.sqrt(HD)
    nt = (((1,), (1,)), ((), ()))
    for b in range(q_ref.shape[0] // sub):
        parts = []
        for j in range(b * sub, (b + 1) * sub):
            ids = ids_ref[j, 0:1, :].astype(jnp.float32).astype(jnp.int32)
            entry = lax.broadcasted_iota(jnp.int32, (entries, tokens), 0)
            onehot = jnp.where(entry == ids, 1.0, 0.0).astype(jnp.bfloat16)
            lookup = lax.dot_general(
                onehot, book_ref[...], (((0,), (0,)), ((), ())), preferred_element_type=jnp.float32
            )
            parts.append((q_ref[j].astype(jnp.float32) + lookup).astype(jnp.bfloat16))
        q = jnp.concatenate(parts, axis=0)
        s1 = lax.dot_general(q, keys, nt, preferred_element_type=jnp.float32)
        s2 = lax.dot_general(q, rk_ref[...], nt, preferred_element_type=jnp.float32)
        live = lax.broadcasted_iota(jnp.int32, s2.shape, 1) < TPF * count_ref[0]
        s2 = jnp.where(live, s2, -1e30)
        top = jnp.maximum(jnp.max(s1, axis=-1, keepdims=True), jnp.max(s2, axis=-1, keepdims=True)) * scale
        p1 = jnp.exp2(s1 * scale - top).astype(jnp.bfloat16)
        p2 = jnp.where(live, jnp.exp2(s2 * scale - top), 0.0).astype(jnp.bfloat16)
        both = jnp.dot(p1, values, preferred_element_type=jnp.float32)
        both = both + jnp.dot(p2, ref_values, preferred_element_type=jnp.float32)
        out = both[:, :HD] / both[:, HD:]
        o_ref[b * sub : (b + 1) * sub] = out.astype(jnp.bfloat16).reshape(sub, tokens, HD)


def attend(tokens, block, count, book, ref_kv):
    n = block.shape[0]
    per, sub = 16, 8
    slots = ref_kv.shape[0]
    return pl.pallas_call(
        lambda *refs: attend_kernel(tokens, sub, *refs),
        grid_spec=pltpu.PrefetchScalarGridSpec(
            num_scalar_prefetch=1,
            grid=(2, n // per),
            in_specs=[
                pl.BlockSpec((per, tokens, HD), lambda h, i, c: (i, 0, h)),
                pl.BlockSpec((n, tokens, HD), lambda h, i, c: (0, 1, h)),
                pl.BlockSpec((n, tokens, HD), lambda h, i, c: (0, 2, h)),
                pl.BlockSpec((per, SIDE, HD), lambda h, i, c: (i, block.shape[1] // SIDE - 1, 0)),
                pl.BlockSpec((book.shape[0], HD), lambda h, i, c: (0, h)),
                pl.BlockSpec((slots, HD), lambda h, i, c: (0, h)),
                pl.BlockSpec((slots, HD), lambda h, i, c: (0, 2 + h)),
            ],
            out_specs=pl.BlockSpec((per, tokens, HD), lambda h, i, c: (i, 0, h)),
        ),
        out_shape=jax.ShapeDtypeStruct((n, tokens, 2 * HD), jnp.bfloat16),
        compiler_params=pltpu.CompilerParams(vmem_limit_bytes=32 << 20),
        cost_estimate=pl.CostEstimate(flops=1 << 10, bytes_accessed=1 << 10, transcendentals=0),
        name="attend",
    )(count, block, block, block, block, book, ref_kv, ref_kv)


def unpack_kernel(r_ref, o_ref, sem):
    width = r_ref.shape[2]
    copies = [
        pltpu.make_async_copy(r_ref.at[d], o_ref.at[:, pl.ds(d * width, width)], sem.at[d])
        for d in range(r_ref.shape[0])
    ]
    for c in copies:
        c.start()
    for c in copies:
        c.wait()


def unpack(received):
    n, tokens, width = received.shape
    return pl.pallas_call(
        unpack_kernel,
        out_shape=jax.ShapeDtypeStruct((tokens, n * width), jnp.bfloat16),
        in_specs=[pl.BlockSpec(memory_space=pl.ANY)],
        out_specs=pl.BlockSpec(memory_space=pl.ANY),
        scratch_shapes=[pltpu.SemaphoreType.DMA((n,))],
        compiler_params=pltpu.CompilerParams(vmem_limit_bytes=1 << 20),
        cost_estimate=pl.CostEstimate(flops=0, bytes_accessed=1 << 10, transcendentals=0),
        name="unpack",
    )(received)


def exchange(x):
    return lax.all_to_all(x, "seq", 0, 0, tiled=True)


def move(block, pairs):
    return lax.ppermute(block, "fsdp", pairs)


def turn(block, step):
    return lax.ppermute(block, "seq", seq_perm(step))


def shards(video_qkv, reference_rows, kv_weight, pose_table, pose_ids, frame_counts):
    tokens = video_qkv.shape[1]
    depth = kv_weight.shape[0]
    video = exchange(pack(jnp.transpose(video_qkv[0], (1, 0, 2)), reference_rows[0], pose_ids))
    codes = jnp.pad(pose_table, ((0, WROWS - depth - pose_table.shape[0]), (0, kv_weight.shape[2])))
    packed = jnp.concatenate([kv_weight.reshape(depth, -1), codes], axis=0)
    column = jnp.concatenate([packed] + [move(packed, pairs) for pairs in Z_MOVES], axis=0)
    ahead, behind = move(column, X_AHEAD), move(column, X_BEHIND)
    far = move(ahead, X_AHEAD)
    own = [column, ahead, far, behind]
    pieces = own + [move(piece, CORE_SWAP) for piece in own]
    weight, book = assemble(pieces, depth)
    video, weight = lax.optimization_barrier((video, weight))
    ref_kv = project(video, weight, reference_rows.shape[1])
    return unpack(exchange(attend(tokens, video, frame_counts, book, ref_kv)))[None]


def solution(mesh):
    placed = (
        P("fsdp", "seq", None, None),
        P("fsdp", "seq", None),
        P("fsdp", None, "seq"),
        P("fsdp", "seq"),
        P("fsdp", "seq"),
        P("fsdp"),
    )
    return jax.shard_map(
        shards, mesh=mesh, in_specs=placed, out_specs=P("fsdp", "seq", None), check_vma=False
    )
```

```python
import math

import jax
import jax.numpy as jnp
from jax import lax
from jax.experimental import pallas as pl
from jax.experimental.pallas import tpu as pltpu
from jax.sharding import PartitionSpec as P

HD = 128
TPF = 16
WROWS = 176
SIDE = 8


def fsdp_perm(move):
    pairs = []
    for i in range(32):
        z, x, c = move(i // 8, i // 2 % 4, i % 2)
        pairs.append((i, z % 4 * 8 + x % 4 * 2 + c))
    return pairs


def direction(core):
    return 1 - 2 * core


Z_MOVES = [fsdp_perm(lambda z, x, c, k=k: (z + k * direction(c), x, c)) for k in (1, 2, 3)]
X_AHEAD = fsdp_perm(lambda z, x, c: (z, x + direction(c), c))
X_BEHIND = fsdp_perm(lambda z, x, c: (z, x - direction(c), c))
CORE_SWAP = fsdp_perm(lambda z, x, c: (z, x, 1 - c))
def pack_kernel(x_ref, rows_hbm, ids_hbm, o_ref, held, rows_ref, ids_ref, side32, side, in_sem, out_sem):
    planes, tokens, _ = held.shape
    n = o_ref.shape[0]
    loads = [pltpu.make_async_copy(x_ref.at[k], held.at[k], in_sem.at[k]) for k in range(planes)]
    loads.append(pltpu.make_async_copy(rows_hbm, rows_ref, in_sem.at[planes]))
    loads.append(pltpu.make_async_copy(ids_hbm, ids_ref, in_sem.at[planes + 1]))
    for load in loads:
        load.start()
    stores = []
    for k in range(planes):
        loads[k].wait()
        for d in range(n):
            part = held.at[k, :, pl.ds(d * 2 * HD, 2 * HD)]
            rows = o_ref.at[d, pl.ds(k * tokens, tokens), :]
            copy = pltpu.make_async_copy(part, rows, out_sem.at[len(stores)])
            copy.start()
            stores.append(copy)
    loads[planes].wait()
    loads[planes + 1].wait()
    x = rows_ref[...].astype(jnp.float32)
    mean = jnp.mean(x, axis=-1, keepdims=True)
    centered = x - mean
    var = jnp.mean(centered * centered, axis=-1, keepdims=True)
    out = centered * lax.rsqrt(var + 1e-06)
    r, width = x.shape
    chunks = width // (2 * HD)
    for c in range(chunks):
        side32[c * r : (c + 1) * r, :] = out[:, c * 2 * HD : (c + 1) * 2 * HD]
    ids = jnp.broadcast_to(ids_ref[...].astype(jnp.float32), (SIDE, tokens))
    side32[chunks * r :, 0:tokens] = ids
    side32[chunks * r :, tokens:] = ids
    side[...] = side32[...].astype(jnp.bfloat16)
    for d in range(n):
        rows = o_ref.at[d, pl.ds(planes * tokens, side.shape[0]), :]
        copy = pltpu.make_async_copy(side, rows, out_sem.at[len(stores)])
        copy.start()
        stores.append(copy)
    for copy in stores:
        copy.wait()


def pack(video, rows, ids):
    planes, tokens, width = video.shape
    n = width // (2 * HD)
    extra = rows.shape[0] * rows.shape[1] // (2 * HD) + SIDE
    return pl.pallas_call(
        pack_kernel,
        out_shape=jax.ShapeDtypeStruct((n, planes * tokens + extra, 2 * HD), jnp.bfloat16),
        in_specs=[pl.BlockSpec(memory_space=pl.ANY)] * 3,
        out_specs=pl.BlockSpec(memory_space=pl.ANY),
        scratch_shapes=[
            pltpu.VMEM(video.shape, jnp.bfloat16),
            pltpu.VMEM(rows.shape, jnp.bfloat16),
            pltpu.VMEM(ids.shape, jnp.int32),
            pltpu.VMEM((extra, 2 * HD), jnp.float32),
            pltpu.VMEM((extra, 2 * HD), jnp.bfloat16),
            pltpu.SemaphoreType.DMA((planes + 2,)),
            pltpu.SemaphoreType.DMA(((planes + 1) * n,)),
        ],
        cost_estimate=pl.CostEstimate(flops=0, bytes_accessed=6 << 20, transcendentals=0),
        name="pack",
    )(video, rows, ids)


def ref_kernel(rows_ref, *refs):
    pieces = refs[:8]
    kv_ref, book_ref, x, split, codes = refs[8:]
    me = lax.axis_index("fsdp")
    mz, mx, mc = me // 8, me // 2 % 4, me % 2
    kdim = split.shape[2]
    n, chunk = rows_ref.shape[0], rows_ref.shape[2]
    r = x.shape[0] // n
    for d in range(n):
        got = rows_ref[d].astype(jnp.float32)
        for c in range(x.shape[1] // chunk):
            x[d * r : (d + 1) * r, c * chunk : (c + 1) * chunk] = got[c * r : (c + 1) * r, :]
    for f in range(32):
        split[f] = x[:, f * kdim : (f + 1) * kdim].astype(jnp.bfloat16)
    total = jnp.zeros(kv_ref.shape, jnp.float32)
    for p in range(8):
        core = mc if p < 4 else 1 - mc
        sign = 1 - 2 * core
        kx = p % 4
        for kz in range(4):
            f = (mz - sign * kz + 4) % 4 * 8 + (mx - sign * kx + 4) % 4 * 2 + core
            row = kz * WROWS
            total = total + jnp.dot(
                split[f], pieces[p][row : row + kdim, :], preferred_element_type=jnp.float32
            )
            codes[pl.ds(pl.multiple_of(f * 8, 8), 8), :] = pieces[p][row + kdim : row + WROWS, 0 : 2 * HD].astype(
                jnp.float32
            )[0:8]
    kv_ref[...] = total.astype(jnp.bfloat16)
    book_ref[...] = codes[...].astype(jnp.bfloat16)


def ref_project(rows, pieces, kdim, depth):
    n = pieces[0].shape[1]
    slots = rows.shape[0] * (rows.shape[1] - SIDE) * rows.shape[2] // depth
    return pl.pallas_call(
        ref_kernel,
        out_shape=(
            jax.ShapeDtypeStruct((slots, n), jnp.bfloat16),
            jax.ShapeDtypeStruct((256, 2 * HD), jnp.bfloat16),
        ),
        in_specs=[pl.BlockSpec(memory_space=pltpu.VMEM)] * 9,
        out_specs=(pl.BlockSpec(memory_space=pltpu.VMEM), pl.BlockSpec(memory_space=pltpu.VMEM)),
        scratch_shapes=[
            pltpu.VMEM((slots, depth), jnp.float32),
            pltpu.VMEM((32, slots, kdim), jnp.bfloat16),
            pltpu.VMEM((256, 2 * HD), jnp.float32),
        ],
        compiler_params=pltpu.CompilerParams(vmem_limit_bytes=16 << 20),
        cost_estimate=pl.CostEstimate(flops=1 << 10, bytes_accessed=1 << 10, transcendentals=0),
        name="ref_project",
    )(rows, *pieces)


def attend_kernel(tokens, sub, count_ref, q_ref, k_ref, v_ref, ids_ref, book_ref, rk_ref, rv_ref, o_ref):
    entries = book_ref.shape[0]
    keys = k_ref[...].reshape(-1, HD)
    values = v_ref[...].reshape(-1, HD)
    ref_values = rv_ref[...]
    values = jnp.concatenate([values, jnp.ones_like(values)], axis=1)
    ref_values = jnp.concatenate([ref_values, jnp.ones_like(ref_values)], axis=1)
    scale = math.log2(math.e) / math.sqrt(HD)
    nt = (((1,), (1,)), ((), ()))
    for b in range(q_ref.shape[0] // sub):
        parts = []
        for j in range(b * sub, (b + 1) * sub):
            ids = ids_ref[j, 0:1, :].astype(jnp.float32).astype(jnp.int32)
            entry = lax.broadcasted_iota(jnp.int32, (entries, tokens), 0)
            onehot = jnp.where(entry == ids, 1.0, 0.0).astype(jnp.bfloat16)
            lookup = lax.dot_general(
                onehot, book_ref[...], (((0,), (0,)), ((), ())), preferred_element_type=jnp.float32
            )
            parts.append((q_ref[j].astype(jnp.float32) + lookup).astype(jnp.bfloat16))
        q = jnp.concatenate(parts, axis=0)
        s1 = lax.dot_general(q, keys, nt, preferred_element_type=jnp.float32)
        s2 = lax.dot_general(q, rk_ref[...], nt, preferred_element_type=jnp.float32)
        live = lax.broadcasted_iota(jnp.int32, s2.shape, 1) < TPF * count_ref[0]
        s2 = jnp.where(live, s2, -1e30)
        top = jnp.maximum(jnp.max(s1, axis=-1, keepdims=True), jnp.max(s2, axis=-1, keepdims=True)) * scale
        p1 = jnp.exp2(s1 * scale - top).astype(jnp.bfloat16)
        p2 = jnp.where(live, jnp.exp2(s2 * scale - top), 0.0).astype(jnp.bfloat16)
        both = jnp.dot(p1, values, preferred_element_type=jnp.float32)
        both = both + jnp.dot(p2, ref_values, preferred_element_type=jnp.float32)
        out = both[:, :HD] / both[:, HD:]
        o_ref[b * sub : (b + 1) * sub] = out.astype(jnp.bfloat16).reshape(sub, tokens, HD)


def attend(tokens, block, rows, count, book, ref_kv):
    n = block.shape[0]
    per, sub = 16, 8
    slots = ref_kv.shape[0]
    return pl.pallas_call(
        lambda *refs: attend_kernel(tokens, sub, *refs),
        grid_spec=pltpu.PrefetchScalarGridSpec(
            num_scalar_prefetch=1,
            grid=(2, n // per),
            in_specs=[
                pl.BlockSpec((per, tokens, HD), lambda h, i, c: (i, 0, h)),
                pl.BlockSpec((n, tokens, HD), lambda h, i, c: (0, 1, h)),
                pl.BlockSpec((n, tokens, HD), lambda h, i, c: (0, 2, h)),
                pl.BlockSpec((per, SIDE, HD), lambda h, i, c: (i, rows.shape[1] // SIDE - 1, 0)),
                pl.BlockSpec((book.shape[0], HD), lambda h, i, c: (0, h)),
                pl.BlockSpec((slots, HD), lambda h, i, c: (0, h)),
                pl.BlockSpec((slots, HD), lambda h, i, c: (0, 2 + h)),
            ],
            out_specs=pl.BlockSpec((per, tokens, HD), lambda h, i, c: (i, 0, h)),
        ),
        out_shape=jax.ShapeDtypeStruct((n, tokens, 2 * HD), jnp.bfloat16),
        compiler_params=pltpu.CompilerParams(vmem_limit_bytes=24 << 20),
        cost_estimate=pl.CostEstimate(flops=1 << 10, bytes_accessed=1 << 10, transcendentals=0),
        name="attend",
    )(count, block, block, block, rows, book, ref_kv, ref_kv)


def unpack_kernel(r_ref, o_ref, sem):
    width = r_ref.shape[2]
    copies = [
        pltpu.make_async_copy(r_ref.at[d], o_ref.at[:, pl.ds(d * width, width)], sem.at[d])
        for d in range(r_ref.shape[0])
    ]
    for c in copies:
        c.start()
    for c in copies:
        c.wait()


def unpack(received):
    n, tokens, width = received.shape
    return pl.pallas_call(
        unpack_kernel,
        out_shape=jax.ShapeDtypeStruct((tokens, n * width), jnp.bfloat16),
        in_specs=[pl.BlockSpec(memory_space=pl.ANY)],
        out_specs=pl.BlockSpec(memory_space=pl.ANY),
        scratch_shapes=[pltpu.SemaphoreType.DMA((n,))],
        compiler_params=pltpu.CompilerParams(vmem_limit_bytes=1 << 20),
        cost_estimate=pl.CostEstimate(flops=0, bytes_accessed=1 << 10, transcendentals=0),
        name="unpack",
    )(received)


def exchange(x):
    return lax.all_to_all(x, "seq", 0, 0, tiled=True)


def move(block, pairs):
    return lax.ppermute(block, "fsdp", pairs)


def turn(block, step):
    return lax.ppermute(block, "seq", seq_perm(step))


def shards(video_qkv, reference_rows, kv_weight, pose_table, pose_ids, frame_counts):
    planes_rows = 3 * video_qkv.shape[1]
    tokens = video_qkv.shape[1]
    depth = kv_weight.shape[0]
    video = exchange(pack(jnp.transpose(video_qkv[0], (1, 0, 2)), reference_rows[0], pose_ids))
    codes = jnp.pad(pose_table, ((0, WROWS - depth - pose_table.shape[0]), (0, kv_weight.shape[2])))
    packed = jnp.concatenate([kv_weight.reshape(depth, -1), codes], axis=0)
    column = jnp.concatenate([packed] + [move(packed, pairs) for pairs in Z_MOVES], axis=0)
    ahead, behind = move(column, X_AHEAD), move(column, X_BEHIND)
    far = move(ahead, X_AHEAD)
    own = [column, ahead, far, behind]
    pieces = own + [move(piece, CORE_SWAP) for piece in own]
    rows = video[:, planes_rows:, :]
    ref_kv, book = ref_project(rows, pieces, depth, reference_rows.shape[2])
    return unpack(exchange(attend(tokens, video, rows, frame_counts, book, ref_kv)))[None]


def solution(mesh):
    placed = (
        P("fsdp", "seq", None, None),
        P("fsdp", "seq", None),
        P("fsdp", None, "seq"),
        P("fsdp", "seq"),
        P("fsdp", "seq"),
        P("fsdp"),
    )
    return jax.shard_map(
        shards, mesh=mesh, in_specs=placed, out_specs=P("fsdp", "seq", None), check_vma=False
    )
```

```python
import math

import jax
import jax.numpy as jnp
from jax import lax
from jax.experimental import pallas as pl
from jax.experimental.pallas import tpu as pltpu
from jax.sharding import PartitionSpec as P

HD = 128
TPF = 16
WROWS = 176
CUTS = 4
SIDE = 8


def fsdp_perm(move):
    pairs = []
    for i in range(32):
        z, x, c = move(i // 8, i // 2 % 4, i % 2)
        pairs.append((i, z % 4 * 8 + x % 4 * 2 + c))
    return pairs


def direction(core):
    return 1 - 2 * core


Z_MOVES = [fsdp_perm(lambda z, x, c, k=k: (z + k * direction(c), x, c)) for k in (1, 2, 3)]
X_AHEAD = fsdp_perm(lambda z, x, c: (z, x + direction(c), c))
X_BEHIND = fsdp_perm(lambda z, x, c: (z, x - direction(c), c))
CORE_SWAP = fsdp_perm(lambda z, x, c: (z, x, 1 - c))
def pack_kernel(x_ref, rows_hbm, ids_hbm, o_ref, held, rows_ref, ids_ref, side32, side, in_sem, out_sem):
    planes, tokens, _ = held.shape
    n = o_ref.shape[0]
    cut = held.shape[2] // CUTS
    loads = []
    for k in range(planes):
        for q in range(CUTS):
            cols = pl.ds(q * cut, cut)
            loads.append(
                pltpu.make_async_copy(x_ref.at[k, :, cols], held.at[k, :, cols], in_sem.at[len(loads)])
            )
    loads.append(pltpu.make_async_copy(rows_hbm, rows_ref, in_sem.at[planes * CUTS]))
    loads.append(pltpu.make_async_copy(ids_hbm, ids_ref, in_sem.at[planes * CUTS + 1]))
    for load in loads:
        load.start()
    stores = []
    for k in range(planes):
        for d in range(n):
            if d % (n // CUTS) == 0:
                loads[k * CUTS + d // (n // CUTS)].wait()
            part = held.at[k, :, pl.ds(d * 2 * HD, 2 * HD)]
            rows = o_ref.at[d, pl.ds(k * tokens, tokens), :]
            copy = pltpu.make_async_copy(part, rows, out_sem.at[len(stores)])
            copy.start()
            stores.append(copy)
    loads[planes * CUTS].wait()
    loads[planes * CUTS + 1].wait()
    x = rows_ref[...].astype(jnp.float32)
    mean = jnp.mean(x, axis=-1, keepdims=True)
    centered = x - mean
    var = jnp.mean(centered * centered, axis=-1, keepdims=True)
    out = centered * lax.rsqrt(var + 1e-06)
    r, width = x.shape
    chunks = width // (2 * HD)
    for c in range(chunks):
        side32[c * r : (c + 1) * r, :] = out[:, c * 2 * HD : (c + 1) * 2 * HD]
    ids = jnp.broadcast_to(ids_ref[...].astype(jnp.float32), (SIDE, tokens))
    side32[chunks * r :, 0:tokens] = ids
    side32[chunks * r :, tokens:] = ids
    side[...] = side32[...].astype(jnp.bfloat16)
    for d in range(n):
        rows = o_ref.at[d, pl.ds(planes * tokens, side.shape[0]), :]
        copy = pltpu.make_async_copy(side, rows, out_sem.at[len(stores)])
        copy.start()
        stores.append(copy)
    for copy in stores:
        copy.wait()


def pack(video, rows, ids):
    planes, tokens, width = video.shape
    n = width // (2 * HD)
    extra = rows.shape[0] * rows.shape[1] // (2 * HD) + SIDE
    return pl.pallas_call(
        pack_kernel,
        out_shape=jax.ShapeDtypeStruct((n, planes * tokens + extra, 2 * HD), jnp.bfloat16),
        in_specs=[pl.BlockSpec(memory_space=pl.ANY)] * 3,
        out_specs=pl.BlockSpec(memory_space=pl.ANY),
        scratch_shapes=[
            pltpu.VMEM(video.shape, jnp.bfloat16),
            pltpu.VMEM(rows.shape, jnp.bfloat16),
            pltpu.VMEM(ids.shape, jnp.int32),
            pltpu.VMEM((extra, 2 * HD), jnp.float32),
            pltpu.VMEM((extra, 2 * HD), jnp.bfloat16),
            pltpu.SemaphoreType.DMA((planes * CUTS + 2,)),
            pltpu.SemaphoreType.DMA(((planes + 1) * n,)),
        ],
        cost_estimate=pl.CostEstimate(flops=0, bytes_accessed=6 << 20, transcendentals=0),
        name="pack",
    )(video, rows, ids)


def ref_kernel(rows_ref, *refs):
    pieces = refs[:8]
    kv_ref, book_ref, x, split, codes = refs[8:]
    me = lax.axis_index("fsdp")
    mz, mx, mc = me // 8, me // 2 % 4, me % 2
    kdim = split.shape[2]
    n, chunk = rows_ref.shape[0], rows_ref.shape[2]
    r = x.shape[0] // n
    for d in range(n):
        got = rows_ref[d].astype(jnp.float32)
        for c in range(x.shape[1] // chunk):
            x[d * r : (d + 1) * r, c * chunk : (c + 1) * chunk] = got[c * r : (c + 1) * r, :]
    for f in range(32):
        split[f] = x[:, f * kdim : (f + 1) * kdim].astype(jnp.bfloat16)
    total = jnp.zeros(kv_ref.shape, jnp.float32)
    for p in range(8):
        core = mc if p < 4 else 1 - mc
        sign = 1 - 2 * core
        kx = p % 4
        for kz in range(4):
            f = (mz - sign * kz + 4) % 4 * 8 + (mx - sign * kx + 4) % 4 * 2 + core
            row = kz * WROWS
            total = total + jnp.dot(
                split[f], pieces[p][row : row + kdim, :], preferred_element_type=jnp.float32
            )
            codes[pl.ds(pl.multiple_of(f * 8, 8), 8), :] = pieces[p][row + kdim : row + WROWS, 0 : 2 * HD].astype(
                jnp.float32
            )[0:8]
    kv_ref[...] = total.astype(jnp.bfloat16)
    book_ref[...] = codes[...].astype(jnp.bfloat16)


def ref_project(rows, pieces, kdim, depth):
    n = pieces[0].shape[1]
    slots = rows.shape[0] * (rows.shape[1] - SIDE) * rows.shape[2] // depth
    return pl.pallas_call(
        ref_kernel,
        out_shape=(
            jax.ShapeDtypeStruct((slots, n), jnp.bfloat16),
            jax.ShapeDtypeStruct((256, 2 * HD), jnp.bfloat16),
        ),
        in_specs=[pl.BlockSpec(memory_space=pltpu.VMEM)] * 9,
        out_specs=(pl.BlockSpec(memory_space=pltpu.VMEM), pl.BlockSpec(memory_space=pltpu.VMEM)),
        scratch_shapes=[
            pltpu.VMEM((slots, depth), jnp.float32),
            pltpu.VMEM((32, slots, kdim), jnp.bfloat16),
            pltpu.VMEM((256, 2 * HD), jnp.float32),
        ],
        compiler_params=pltpu.CompilerParams(vmem_limit_bytes=16 << 20),
        cost_estimate=pl.CostEstimate(flops=1 << 10, bytes_accessed=1 << 10, transcendentals=0),
        name="ref_project",
    )(rows, *pieces)


def attend_kernel(tokens, sub, count_ref, q_ref, k_ref, v_ref, ids_ref, book_ref, rk_ref, rv_ref, o_ref):
    entries = book_ref.shape[0]
    keys = k_ref[...].reshape(-1, HD)
    values = v_ref[...].reshape(-1, HD)
    ref_values = rv_ref[...]
    values = jnp.concatenate([values, jnp.ones_like(values)], axis=1)
    ref_values = jnp.concatenate([ref_values, jnp.ones_like(ref_values)], axis=1)
    scale = math.log2(math.e) / math.sqrt(HD)
    nt = (((1,), (1,)), ((), ()))
    for b in range(q_ref.shape[0] // sub):
        parts = []
        for j in range(b * sub, (b + 1) * sub):
            ids = ids_ref[j, 0:1, :].astype(jnp.float32).astype(jnp.int32)
            entry = lax.broadcasted_iota(jnp.int32, (entries, tokens), 0)
            onehot = jnp.where(entry == ids, 1.0, 0.0).astype(jnp.bfloat16)
            lookup = lax.dot_general(
                onehot, book_ref[...], (((0,), (0,)), ((), ())), preferred_element_type=jnp.float32
            )
            parts.append((q_ref[j].astype(jnp.float32) + lookup).astype(jnp.bfloat16))
        q = jnp.concatenate(parts, axis=0)
        s1 = lax.dot_general(q, keys, nt, preferred_element_type=jnp.float32)
        s2 = lax.dot_general(q, rk_ref[...], nt, preferred_element_type=jnp.float32)
        live = lax.broadcasted_iota(jnp.int32, s2.shape, 1) < TPF * count_ref[0]
        s2 = jnp.where(live, s2, -1e30)
        top = jnp.maximum(jnp.max(s1, axis=-1, keepdims=True), jnp.max(s2, axis=-1, keepdims=True)) * scale
        p1 = jnp.exp2(s1 * scale - top).astype(jnp.bfloat16)
        p2 = jnp.where(live, jnp.exp2(s2 * scale - top), 0.0).astype(jnp.bfloat16)
        both = jnp.dot(p1, values, preferred_element_type=jnp.float32)
        both = both + jnp.dot(p2, ref_values, preferred_element_type=jnp.float32)
        out = both[:, :HD] / both[:, HD:]
        o_ref[b * sub : (b + 1) * sub] = out.astype(jnp.bfloat16).reshape(sub, tokens, HD)


def attend(tokens, block, rows, count, book, ref_kv):
    n = block.shape[0]
    per, sub = 16, 8
    slots = ref_kv.shape[0]
    return pl.pallas_call(
        lambda *refs: attend_kernel(tokens, sub, *refs),
        grid_spec=pltpu.PrefetchScalarGridSpec(
            num_scalar_prefetch=1,
            grid=(2, n // per),
            in_specs=[
                pl.BlockSpec((per, tokens, HD), lambda h, i, c: (i, 0, h)),
                pl.BlockSpec((n, tokens, HD), lambda h, i, c: (0, 1, h)),
                pl.BlockSpec((n, tokens, HD), lambda h, i, c: (0, 2, h)),
                pl.BlockSpec((per, SIDE, HD), lambda h, i, c: (i, rows.shape[1] // SIDE - 1, 0)),
                pl.BlockSpec((book.shape[0], HD), lambda h, i, c: (0, h)),
                pl.BlockSpec((slots, HD), lambda h, i, c: (0, h)),
                pl.BlockSpec((slots, HD), lambda h, i, c: (0, 2 + h)),
            ],
            out_specs=pl.BlockSpec((per, tokens, HD), lambda h, i, c: (i, 0, h)),
        ),
        out_shape=jax.ShapeDtypeStruct((n, tokens, 2 * HD), jnp.bfloat16),
        compiler_params=pltpu.CompilerParams(vmem_limit_bytes=24 << 20),
        cost_estimate=pl.CostEstimate(flops=1 << 10, bytes_accessed=1 << 10, transcendentals=0),
        name="attend",
    )(count, block, block, block, rows, book, ref_kv, ref_kv)


def unpack_kernel(r_ref, o_ref, sem):
    width = r_ref.shape[2]
    copies = [
        pltpu.make_async_copy(r_ref.at[d], o_ref.at[:, pl.ds(d * width, width)], sem.at[d])
        for d in range(r_ref.shape[0])
    ]
    for c in copies:
        c.start()
    for c in copies:
        c.wait()


def unpack(received):
    n, tokens, width = received.shape
    return pl.pallas_call(
        unpack_kernel,
        out_shape=jax.ShapeDtypeStruct((tokens, n * width), jnp.bfloat16),
        in_specs=[pl.BlockSpec(memory_space=pl.ANY)],
        out_specs=pl.BlockSpec(memory_space=pl.ANY),
        scratch_shapes=[pltpu.SemaphoreType.DMA((n,))],
        compiler_params=pltpu.CompilerParams(vmem_limit_bytes=1 << 20),
        cost_estimate=pl.CostEstimate(flops=0, bytes_accessed=1 << 10, transcendentals=0),
        name="unpack",
    )(received)


def exchange(x):
    return lax.all_to_all(x, "seq", 0, 0, tiled=True)


def move(block, pairs):
    return lax.ppermute(block, "fsdp", pairs)


def turn(block, step):
    return lax.ppermute(block, "seq", seq_perm(step))


def shards(video_qkv, reference_rows, kv_weight, pose_table, pose_ids, frame_counts):
    planes_rows = 3 * video_qkv.shape[1]
    tokens = video_qkv.shape[1]
    depth = kv_weight.shape[0]
    video = exchange(pack(jnp.transpose(video_qkv[0], (1, 0, 2)), reference_rows[0], pose_ids))
    codes = jnp.pad(pose_table, ((0, WROWS - depth - pose_table.shape[0]), (0, kv_weight.shape[2])))
    packed = jnp.concatenate([kv_weight.reshape(depth, -1), codes], axis=0)
    column = jnp.concatenate([packed] + [move(packed, pairs) for pairs in Z_MOVES], axis=0)
    ahead, behind = move(column, X_AHEAD), move(column, X_BEHIND)
    far = move(ahead, X_AHEAD)
    own = [column, ahead, far, behind]
    pieces = own + [move(piece, CORE_SWAP) for piece in own]
    rows = video[:, planes_rows:, :]
    ref_kv, book = ref_project(rows, pieces, depth, reference_rows.shape[2])
    return unpack(exchange(attend(tokens, video, rows, frame_counts, book, ref_kv)))[None]


def solution(mesh):
    placed = (
        P("fsdp", "seq", None, None),
        P("fsdp", "seq", None),
        P("fsdp", None, "seq"),
        P("fsdp", "seq"),
        P("fsdp", "seq"),
        P("fsdp"),
    )
    return jax.shard_map(
        shards, mesh=mesh, in_specs=placed, out_specs=P("fsdp", "seq", None), check_vma=False
    )
```
